32 devices in a mesh: group: 2 (over y), tile: 4 (over x, core), seq: 4 (over z).
Axes of the slice: x: 2, y: 2, z: 4, core: 2. Of those that a mesh axis runs over, the one named last changes fastest.
Arguments:
- hidden: bfloat16 [8, 1024, 3072], P(('group', 'tile'), 'seq'), parts along dimension 0
- modulation: float32 [10, 3072], P('group'), parts along dimension 0, may hold values from -3 to 3
- w_qkv: bfloat16 [3072, 9216], P('tile', 'seq')
- w_out: bfloat16 [3072, 3072], P('seq', 'tile'), may hold values from -0.109375 to 0.109375
- w_head: bfloat16 [3072, 64], replicated, may hold values from -0.109375 to 0.109375
- latent: float32 [8, 1024, 64], P(('group', 'tile'), 'seq'), parts along dimension 0, may hold values from -6 to 6
- weights_int: int32 [8, 1024], P(('group', 'tile'), 'seq'), parts along dimension 0, may hold values from 1 to 8
- step_index: int32 [2], P('group'), parts along dimension 0, may hold values from 0 to 13
Outputs:
- stepped: float32 [8, 1024, 64], P(('group', 'tile'), 'seq'), parts along dimension 0
- clean: float32 [8, 1024, 64], P(('group', 'tile'), 'seq'), parts along dimension 0
The draws below stay inside these ranges and needn't reach their ends.
There are 2 independent parts, one for each index of `group`. The reference program is written for one: setup_inputs(seed, part) draws one part's arguments, and reference() takes and returns one part's arrays. A program takes and returns all parts, laid end to end along the dimension named above; an argument that names none is the same for every part. Nothing has to cross between parts.
All inputs are finite; a program needn't handle non-finite values.
Results may differ from the reference program's by a relative error of at most 0.0055.
Values may be sent and summed in bfloat16 or wider, within the bound.
A program may use at most 64 MiB of HBM per device.

```python
import math
import jax
import jax.numpy as jnp
from jax import lax

D = 3072
HEADS = 24
HD = 128
C = 64
TILE_LEN = 1024
NSTEPS = 28
TILES = 4
STRIDE = 512
N_SEQ = 4


def draw_hidden(key, part):
    first = jax.random.fold_in(key, 0)
    second = jax.random.fold_in(key, 1)
    third = jax.random.fold_in(key, 2)
    fifth = jax.random.fold_in(key, 4)
    sixth = jax.random.fold_in(key, 5)
    clusters = 16
    rows = jnp.exp(jax.random.uniform(second, (TILES, TILE_LEN, 1), jnp.float32, math.log(0.3), math.log(3.0)))
    cols = jnp.exp(jax.random.uniform(third, (1, 1, D), jnp.float32, math.log(0.3), math.log(3.0)))
    labels = jax.random.randint(fifth, (TILES, TILE_LEN, 1), 0, clusters)
    centres = jax.random.normal(sixth, (TILES, clusters, D), jnp.float32)
    noise = jax.random.normal(first, (TILES, TILE_LEN, D), jnp.float32)
    picked = jnp.take_along_axis(centres, labels, axis=1)
    base = 0.9 * picked + 0.45 * noise
    base = jnp.clip(base, -5.0, 5.0)
    return (base * rows * cols).astype(jnp.bfloat16)


def draw_w_qkv(key, part):
    first, second = jax.random.split(jax.random.fold_in(key, 17), 2)
    scale = 1.0 / math.sqrt(D)
    base = jax.random.normal(first, (D, HEADS, 3, HD), jnp.float32) * scale
    extra = jax.random.normal(second, (D, HEADS, HD), jnp.float32) * scale
    keys = 0.6 * base[:, :, 0] + 0.8 * extra
    stacked = jnp.stack([base[:, :, 0], keys, base[:, :, 2]], axis=2)
    return stacked.reshape(D, 3 * D).astype(jnp.bfloat16)


def set_ends(values, stream_key, least, top_value):
    dims = values.shape
    index_at = [jax.random.randint(jax.random.fold_in(stream_key, axis), (), 0, dims[axis]) for axis in range(len(dims))]
    values = values.at[tuple(index_at)].set(least)
    longest = dims.index(max(dims))
    index_at[longest] = (index_at[longest] + 1) % dims[longest]
    return values.at[tuple(index_at)].set(top_value)


def level_of(key, extent, cuts, least, top_value):
    def one(axis_at, blocks):
        steps = jax.random.uniform(jax.random.fold_in(jax.random.fold_in(key, 6), axis_at), (blocks,), jnp.float32, least / len(cuts), top_value / len(cuts))
        return jnp.repeat(jnp.exp(steps), extent[axis_at] // blocks).reshape((-1,) + (1,) * (len(extent) - axis_at - 1))

    gain = one(*cuts[0])
    for cut in cuts[1:]:
        gain = gain * one(*cut)
    return gain


def normal_values(own_key, dims, width, most, pieces=(), held_as=jnp.bfloat16):
    result = width * jax.random.normal(own_key, dims, jnp.float32)
    if pieces:
        result = result * level_of(own_key, dims, pieces, -0.22, 0.18)
    return jnp.clip(result, -most, most).astype(held_as)


def setup_inputs(seed: int = 0, part: int = 0) -> dict:
    streams_of = jax.random.split(jax.random.key(seed), 9)
    part_splits = jax.random.split(jax.random.fold_in(streams_of[8], part), 9)
    return {
        "hidden": draw_hidden(jax.random.fold_in(jax.random.fold_in(streams_of[8], part), 71), part),
        "modulation": normal_values(part_splits[1], (5, D), 0.5, 3.0, (), jnp.float32),
        "w_qkv": draw_w_qkv(jax.random.fold_in(streams_of[8], 71), part),
        "w_out": normal_values(streams_of[3], (D, D), D ** -0.5, 0.109375, ((0, 4), (1, 4))),
        "w_head": normal_values(streams_of[4], (D, C), D ** -0.5, 0.109375),
        "latent": normal_values(part_splits[5], (TILES, TILE_LEN, C), 1.0, 6.0, ((0, 4), (1, 4)), jnp.float32),
        "weights_int": set_ends(jax.random.randint(part_splits[6], (TILES, TILE_LEN), 1, 9), jax.random.fold_in(part_splits[6], 1), 1, 8).astype(jnp.int32),
        "step_index": jax.random.randint(part_splits[7], (1,), 0, NSTEPS // 2).astype(jnp.int32),
    }


def layer_norm(values):
    mean = lax.optimization_barrier(jnp.mean(values, axis=-1, keepdims=True))
    centred = values - mean
    spread = lax.optimization_barrier(jnp.mean(centred * centred, axis=-1, keepdims=True))
    return centred * lax.rsqrt(spread + 1e-06)

def root_norm(values):
    return values * lax.rsqrt(lax.optimization_barrier(jnp.mean(values * values, axis=-1, keepdims=True)) + 1e-06)

def noise_level(index, steps):
    level = 1.0 - index / steps
    return 3.0 * level / (1.0 + 2.0 * level)

def reference(hidden, modulation, w_qkv, w_out, w_head, latent, weights_int, step_index):
    qkv_full = w_qkv.astype(jnp.float32)
    out_groups = w_out.astype(jnp.float32).reshape(N_SEQ, D // N_SEQ, D)
    head_full = w_head.astype(jnp.float32)

    def one_tile(tokens):
        local = tokens.astype(jnp.float32)
        norm_in = (layer_norm(local) * (1.0 + modulation[1]) + modulation[0]).astype(jnp.bfloat16)
        proj = jnp.dot(norm_in.astype(jnp.float32), qkv_full)
        proj = proj.reshape(TILE_LEN, HEADS, 3, HD)
        queries = root_norm(proj[:, :, 0]).astype(jnp.bfloat16).astype(jnp.float32)
        keys = root_norm(proj[:, :, 1]).astype(jnp.bfloat16).astype(jnp.float32)
        values = proj[:, :, 2].astype(jnp.bfloat16).astype(jnp.float32)
        scores = jnp.einsum('qhe,khe->hqk', queries, keys) / math.sqrt(HD)
        expo = jnp.exp(scores)
        probs = (expo / lax.optimization_barrier(jnp.sum(expo, axis=-1, keepdims=True))).astype(jnp.bfloat16).astype(jnp.float32)
        attended = jnp.einsum('hqk,khe->qhe', probs, values).astype(jnp.bfloat16)
        attended = attended.astype(jnp.float32).reshape(TILE_LEN, N_SEQ, D // N_SEQ)
        parts = jnp.einsum('lgd,gdo->glo', attended, out_groups).astype(jnp.bfloat16)
        summed = lax.optimization_barrier(jnp.sum(parts.astype(jnp.float32), axis=0))
        mixed = local + modulation[2] * summed
        norm_out = (layer_norm(mixed) * (1.0 + modulation[4]) + modulation[3]).astype(jnp.bfloat16)
        return jnp.dot(norm_out.astype(jnp.float32), head_full)
    velocity = lax.map(one_tile, hidden)
    index = step_index[0].astype(jnp.float32)
    now = noise_level(index, NSTEPS)
    after = noise_level(index + 1.0, NSTEPS)
    moved = latent + (after - now) * velocity
    guess = latent - now * velocity
    weight = weights_int.astype(jnp.float32)
    band = (TILES - 1) * STRIDE + TILE_LEN
    places = (jnp.arange(TILES, dtype=jnp.int32)[:, None] * STRIDE + jnp.arange(TILE_LEN, dtype=jnp.int32)[None, :]).reshape(-1)
    stacked = jnp.concatenate([moved, guess], axis=2) * weight[:, :, None]
    totals = jnp.zeros((band, 2 * C), jnp.float32).at[places].add(stacked.reshape(-1, 2 * C))
    norms = jnp.zeros((band,), jnp.float32).at[places].add(weight.reshape(-1))
    joined = (totals[places] / norms[places][:, None]).reshape(TILES, TILE_LEN, 2 * C)
    return (joined[:, :, :C], joined[:, :, C:])
```

```python
import functools
import math

import jax
import jax.numpy as jnp
from jax import lax
from jax.experimental import pallas as pl
from jax.experimental.pallas import tpu as pltpu
from jax.sharding import PartitionSpec as P

HD = 128
NSTEPS = 28


def layer_norm(values):
    mean = jnp.mean(values, axis=-1, keepdims=True)
    centred = values - mean
    spread = jnp.mean(centred * centred, axis=-1, keepdims=True)
    return centred * lax.rsqrt(spread + 1e-06)


def root_norm(values):
    return values * lax.rsqrt(jnp.mean(values * values, axis=-1, keepdims=True) + 1e-06)


def noise_level(index, steps):
    level = 1.0 - index / steps
    return 3.0 * level / (1.0 + 2.0 * level)


MESH = pl.DeviceIdType.MESH


def run(cond, body):
    if cond is None:
        body()
    else:
        pl.when(cond)(body)


def arrives(place, count, way, far):
    return place >= far if way == 0 else place <= count - 1 - far


def goes_on(place, count, way):
    return place < count - 1 if way == 0 else place > 0


def gather_kernel(
    groups, chips, seqs, scale, norm, wq, wo, q_all, o_all, attended,
    n_all, v_wq, v_wo, w_head, queries, keys, values, local, w_sem,
    nz_s, nz_r, oz_s, oz_r, qx_s, qx_r, ox_s, ox_r, qy_s, qy_r, oy_s, oy_r, qc_s, qc_r, oc_s, oc_r,
):
    group, tile, place = lax.axis_index("group"), lax.axis_index("tile"), lax.axis_index("seq")
    chip, core = tile // 2, tile % 2
    other = 1 - core
    partner = {"tile": chip * 2 + other}
    q_rows, o_rows = wq.shape[0] // groups, wo.shape[0] // groups
    both = jnp.logical_and

    def q_part(owner, part):
        return q_all.at[owner, pl.ds(pl.multiple_of(part * q_rows, 8), q_rows)]

    def o_part(owner, row, part):
        return o_all.at[owner, row, pl.ds(pl.multiple_of(part * o_rows, 8), o_rows)]

    def along_seq(way):
        return {"seq": place + 1 - 2 * way}

    def along_chip(way):
        return {"tile": tile + 2 - 4 * way}

    def peer(step):
        return {"group": (group + step) % groups}

    barrier = pltpu.get_barrier_semaphore()
    greet = [(goes_on(place, seqs, way), along_seq(way)) for way in (0, 1)]
    greet += [(goes_on(chip, chips, way), along_chip(way)) for way in (0, 1)]
    greet += [(None, peer(step)) for step in range(1, groups)] + [(None, partner)]
    for cond, device in greet:
        run(cond, lambda device=device: pl.semaphore_signal(barrier, inc=1, device_id=device, device_id_type=MESH))
    met = groups + sum(goes_on(at, count, way).astype(jnp.int32) for at, count in ((place, seqs), (chip, chips)) for way in (0, 1))
    pl.semaphore_wait(barrier, met)

    sent = []

    def copy(source, target, send, recv, device):
        return pltpu.make_async_remote_copy(
            src_ref=source, dst_ref=target, send_sem=send, recv_sem=recv, device_id=device, device_id_type=MESH
        )

    def start(cond, *made):
        run(cond, lambda: copy(*made).start())
        sent.append((cond, made))

    def arrived(cond, target, send, recv, device):
        run(cond, lambda: copy(target, target, send, recv, device).wait_recv())

    def q_to_peers(cond, at, source):
        for step in range(1, groups):
            start(cond, source, q_part(at * 2 + core, group), qy_s.at[at, step], qy_r.at[at, step], peer(step))

    def q_to_partner(cond, at, part, source):
        start(cond, source, q_part(at * 2 + core, part), qc_s.at[at, part], qc_r.at[at, part], partner)

    def o_to_peers(cond, at, row, source):
        for step in range(1, groups):
            start(cond, source, o_part(at * 2 + core, row, group), oy_s.at[at, row, step], oy_r.at[at, row, step], peer(step))

    def o_to_partner(cond, at, row, part, source):
        start(cond, source, o_part(at * 2 + core, row, part), oc_s.at[at, row, part], oc_r.at[at, row, part], partner)

    def o_along_chip(cond, way, far, at, row, source):
        start(cond, source, o_part(at * 2 + core, row, group), ox_s.at[way, far, row], ox_r.at[way, far, row], along_chip(way))

    loads = [pltpu.make_async_copy(a, b, local.at[k]) for k, (a, b) in enumerate(((norm, n_all.at[place]), (wq, v_wq), (wo, v_wo)))]
    for load in loads:
        load.start()

    own_q = wq.at[pl.ds(pl.multiple_of(group * q_rows, 8), q_rows)]
    own_o = wo.at[pl.ds(pl.multiple_of(group * o_rows, 8), o_rows)]
    for way in (0, 1):
        go = goes_on(place, seqs, way)
        start(go, norm, n_all.at[place], nz_s.at[way, 1], nz_r.at[way, 1], along_seq(way))
        start(go, own_o, o_part(tile, place, group), oz_s.at[way, 1], oz_r.at[way, 1], along_seq(way))
        go = goes_on(chip, chips, way)
        start(go, own_q, q_part(tile, group), qx_s.at[way, 1], qx_r.at[way, 1], along_chip(way))
        o_along_chip(go, way, 1, chip, place, own_o)
    for part in range(groups):
        q_to_partner(None, chip, part, wq.at[pl.ds(part * q_rows, q_rows)])
        o_to_partner(None, chip, place, part, wo.at[pl.ds(part * o_rows, o_rows)])

    stores = [pltpu.make_async_copy(b, a, local.at[k]) for k, (a, b) in enumerate(((q_all.at[tile], v_wq), (o_all.at[tile, place], v_wo)))]
    for load in loads:
        load.wait()
    for store in stores:
        store.start()

    def rows_from_chips(rows):
        for far in range(1, chips):
            for way in (0, 1):
                at = chip - far if way == 0 else chip + far
                for given, row in rows:
                    here = arrives(chip, chips, way, far)
                    here = here if given is None else both(here, given)
                    piece = o_part(at * 2 + core, row, group)
                    arrived(here, piece, ox_s.at[way, far, row], ox_r.at[way, far, row], along_chip(way))
                    if far < chips - 1:
                        o_along_chip(both(here, goes_on(chip, chips, way)), way, far + 1, at, row, piece)
                    o_to_peers(here, at, row, piece)
                    o_to_partner(here, at, row, group, piece)

    def rows_at(far):
        if far == 0:
            return [(None, place)]
        return [(arrives(place, seqs, way, far), place - far if way == 0 else place + far) for way in (0, 1)]

    def out_step(far):
        for way in (0, 1):
            here = arrives(place, seqs, way, far)
            row = place - far if way == 0 else place + far
            piece = o_part(tile, row, group)
            arrived(here, piece, oz_s.at[way, far], oz_r.at[way, far], along_seq(way))
            if far < seqs - 1:
                start(both(here, goes_on(place, seqs, way)), piece, piece, oz_s.at[way, far + 1], oz_r.at[way, far + 1], along_seq(way))
            for side in (0, 1):
                o_along_chip(both(here, goes_on(chip, chips, side)), side, 1, chip, row, piece)
            o_to_peers(here, chip, row, piece)
            o_to_partner(here, chip, row, group, piece)

    def norm_step(far):
        for way in (0, 1):
            here = arrives(place, seqs, way, far)
            row = place - far if way == 0 else place + far
            piece = n_all.at[row]
            arrived(here, piece, nz_s.at[way, far], nz_r.at[way, far], along_seq(way))
            if far < seqs - 1:
                start(both(here, goes_on(place, seqs, way)), piece, piece, nz_s.at[way, far + 1], nz_r.at[way, far + 1], along_seq(way))

    def chip_step(far):
        for way in (0, 1):
            here = arrives(chip, chips, way, far)
            at = chip - far if way == 0 else chip + far
            piece = q_part(at * 2 + core, group)
            arrived(here, piece, qx_s.at[way, far], qx_r.at[way, far], along_chip(way))
            if far < chips - 1:
                start(both(here, goes_on(chip, chips, way)), piece, piece, qx_s.at[way, far + 1], qx_r.at[way, far + 1], along_chip(way))
            q_to_peers(here, at, piece)
            q_to_partner(here, at, group, piece)

    def q_from_peers():
        for step in range(1, groups):
            part = (group + groups - step) % groups
            for at in range(chips):
                away = chip != at
                piece = q_part(at * 2 + core, part)
                arrived(away, piece, qy_s.at[at, step], qy_r.at[at, step], partner)
                q_to_partner(away, at, part, piece)

    def o_from_peers():
        for step in range(1, groups):
            part = (group + groups - step) % groups
            for at in range(chips):
                for row in range(seqs):
                    away = jnp.logical_or(chip != at, place != row)
                    piece = o_part(at * 2 + core, row, part)
                    arrived(away, piece, oy_s.at[at, row, step], oy_r.at[at, row, step], partner)
                    o_to_partner(away, at, row, part, piece)

    last = max(chips, seqs) - 1
    for far in range(1, last + 1):
        if 1 < far < seqs:
            rows_from_chips(rows_at(far - 1))
        if far < seqs:
            norm_step(far)
        if far < seqs - 1:
            out_step(far)
        if far < chips:
            chip_step(far)
        if far == 1 and seqs > 1:
            rows_from_chips(rows_at(0))
        if far == max(chips - 1, min(2, last)):
            q_from_peers()
    for at in range(chips):
        for part in range(groups):
            arrived(None, q_part(at * 2 + other, part), qc_s.at[at, part], qc_r.at[at, part], partner)
    for store in stores:
        store.wait()

    heads = wq.shape[1] // (3 * HD)
    depth, block = wq.shape[0], norm.shape[0]

    def fetch(head):
        slot = head % 2
        columns = pl.ds(pl.multiple_of(head * (3 * HD), 128), 3 * HD)
        return [
            pltpu.make_async_copy(
                q_all.at[at, :, columns], w_head.at[slot, pl.ds(at * depth, depth)], w_sem.at[slot, at]
            )
            for at in range(2 * chips)
        ]

    def one_head(head, carry):
        for load in fetch(head):
            load.wait()

        @pl.when(head + 1 < heads)
        def _():
            for load in fetch(head + 1):
                load.start()

        weights = w_head.at[head % 2]
        for row in range(seqs):
            at = pl.ds(row * block, block)
            part = jnp.dot(n_all[row], weights[...], preferred_element_type=jnp.float32)
            queries[at, :] = root_norm(part[:, :HD]).astype(jnp.bfloat16)
            keys[at, :] = root_norm(part[:, HD : 2 * HD]).astype(jnp.bfloat16)
            values[at, :] = part[:, 2 * HD :].astype(jnp.bfloat16)
        for row in range(seqs):
            at = pl.ds(row * block, block)
            scores = lax.dot_general(
                queries[at, :], keys[...], (((1,), (1,)), ((), ())), preferred_element_type=jnp.float32
            )
            expo = jnp.exp(scores * scale)
            probs = (expo * (1.0 / jnp.sum(expo, axis=-1, keepdims=True))).astype(jnp.bfloat16)
            attended[at, pl.ds(pl.multiple_of(head * HD, 128), HD)] = jnp.dot(
                probs, values[...], preferred_element_type=jnp.float32
            ).astype(jnp.bfloat16)
        return carry

    def between(step):
        if step == 0 and seqs > 1:
            out_step(seqs - 1)
        if step == 1:
            rows_from_chips(rows_at(seqs - 1))
        if step == 2:
            o_from_peers()

    for load in fetch(0):
        load.start()
    cuts = [0, heads // 3, heads // 2, 5 * heads // 6, heads]
    for step in range(4):
        if cuts[step] < cuts[step + 1]:
            lax.fori_loop(cuts[step], cuts[step + 1], one_head, 0)
        between(step)

    for at in range(chips):
        for part in range(groups):
            for row in range(seqs):
                arrived(None, o_part(at * 2 + other, row, part), oc_s.at[at, row, part], oc_r.at[at, row, part], partner)
    for cond, made in sent:
        run(cond, lambda made=made: copy(*made).wait_send())


def gather(norm, wq, wo):
    groups, tiles, seqs = (lax.axis_size(name) for name in ("group", "tile", "seq"))
    chips = tiles // 2
    length = seqs * norm.shape[0]
    pairs = [(2, seqs), (2, seqs), (2, chips), (2, chips, seqs), (chips, groups), (chips, seqs, groups), (chips, groups), (chips, seqs, groups)]
    return pl.pallas_call(
        functools.partial(gather_kernel, groups, chips, seqs, 1.0 / math.sqrt(HD)),
        out_shape=(
            jax.ShapeDtypeStruct((tiles,) + wq.shape, wq.dtype),
            jax.ShapeDtypeStruct((tiles, seqs) + wo.shape, wo.dtype),
            jax.ShapeDtypeStruct((length, wq.shape[1] // 3), norm.dtype),
        ),
        in_specs=[pl.BlockSpec(memory_space=pl.ANY)] * 3,
        out_specs=(pl.BlockSpec(memory_space=pl.ANY),) * 2 + (pl.BlockSpec(memory_space=pltpu.VMEM),),
        scratch_shapes=[pltpu.VMEM((seqs,) + norm.shape, norm.dtype)]
        + [pltpu.VMEM(a.shape, a.dtype) for a in (wq, wo)]
        + [pltpu.VMEM((2, tiles * wq.shape[0], 3 * HD), wq.dtype)]
        + [pltpu.VMEM((length, HD), norm.dtype)] * 3
        + [pltpu.SemaphoreType.DMA((3,)), pltpu.SemaphoreType.DMA((2, tiles))]
        + [pltpu.SemaphoreType.DMA(shape) for shape in pairs for _ in range(2)],
        compiler_params=pltpu.CompilerParams(collective_id=0, has_side_effects=True),
    )(norm, wq, wo)


def tail_kernel(attended, blocks, hidden, modulation, w_head, velocity, summed):
    at = pl.program_id(0)
    width = blocks.shape[2]
    here = pl.ds(pl.multiple_of(at * width, 128), width)
    summed[:, here] = jnp.dot(attended[...], blocks[0], preferred_element_type=jnp.float32)

    @pl.when(at == pl.num_programs(0) - 1)
    def _():
        mixed = hidden[...].astype(jnp.float32) + modulation[2:3] * summed[...]
        norm_out = (layer_norm(mixed) * (1.0 + modulation[4:5]) + modulation[3:4]).astype(jnp.bfloat16)
        velocity[...] = jnp.dot(norm_out, w_head[...], preferred_element_type=jnp.float32)


def tail(attended, blocks, hidden, modulation, w_head):
    tiles, depth, width = blocks.shape
    if width % 128:
        summed = jnp.concatenate(
            [jnp.dot(attended, blocks[at], preferred_element_type=jnp.float32) for at in range(tiles)], axis=1
        )
        mixed = hidden.astype(jnp.float32) + modulation[2] * summed
        norm_out = (layer_norm(mixed) * (1.0 + modulation[4]) + modulation[3]).astype(jnp.bfloat16)
        return jnp.dot(norm_out, w_head, preferred_element_type=jnp.float32)
    whole = [pl.BlockSpec(a.shape, lambda at: (0, 0), pipeline_mode=pl.Buffered(1)) for a in (attended, hidden, modulation, w_head)]
    return pl.pallas_call(
        tail_kernel,
        grid=(tiles,),
        out_shape=jax.ShapeDtypeStruct((hidden.shape[0], w_head.shape[1]), jnp.float32),
        in_specs=[whole[0], pl.BlockSpec((1, depth, width), lambda at: (at, 0, 0)), *whole[1:]],
        out_specs=pl.BlockSpec((hidden.shape[0], w_head.shape[1]), lambda at: (0, 0)),
        scratch_shapes=[pltpu.VMEM(hidden.shape, jnp.float32)],
    )(attended, blocks, hidden, modulation, w_head)


def step_kernel(
    scale, hidden, wq, wo, modulation, w_head, velocity,
    n_all, normed, w_all, queries, keys, values, attended, att_in, o_all, summed, vel, vel_in, local,
    nz_s, nz_r, qx_s, qx_r, qy_s, qy_r, qc_s, qc_r, qo_s, qo_r, oz_s, oz_r, ox_s, ox_r, oy_s, oy_r, oc_s, oc_r,
    at_s, at_r, vl_s, vl_r,
):
    group, tile, place = lax.axis_index("group"), lax.axis_index("tile"), lax.axis_index("seq")
    seqs, block, width = n_all.shape
    chip, core = tile // 2, tile % 2
    side = place // 2
    toward = 1 - 2 * side
    inner = jnp.logical_or(place == 1, place == 2)
    outer_end = jnp.logical_not(inner)
    over = (1 - chip) * 2 + core
    mate = chip * 2 + 1 - core
    mate_over = (1 - chip) * 2 + 1 - core
    x_dev, y_dev, p_dev, in_dev = {"tile": over}, {"group": 1 - group}, {"tile": mate}, {"seq": place + toward}
    out_dev = {"seq": place - toward}
    depth, cols = wq.shape
    q_half, o_half = depth // 2, wo.shape[0] // 2
    chunks = qx_s.shape[0]
    piece = q_half // chunks
    pairs = attended.shape[0]
    heads = queries.shape[0]
    both = jnp.logical_and

    def yes():
        return None

    def middle():
        return inner

    def ends():
        return outer_end

    def along(way):
        return {"seq": place + 1 - 2 * way}

    barrier = pltpu.get_barrier_semaphore()
    greet = [x_dev, y_dev, p_dev] + [{"seq": (place + far) % seqs} for far in range(1, seqs)]
    for device in greet:
        pl.semaphore_signal(barrier, inc=1, device_id=device, device_id_type=MESH)
    pl.semaphore_wait(barrier, len(greet))

    sent = []

    def copy(source, target, send, recv, device):
        return pltpu.make_async_remote_copy(
            src_ref=source, dst_ref=target, send_sem=send, recv_sem=recv, device_id=device, device_id_type=MESH
        )

    def start(cond, make):
        run(cond(), lambda: copy(*make()).start())
        sent.append((cond, make))

    def arrived(cond, target, recv):
        run(cond, lambda: copy(target(), target(), recv, recv, p_dev).wait_recv())

    def w_rows(owner, part, at):
        return w_all.at[pl.ds(pl.multiple_of(owner * depth + part * q_half + at * piece, 16), piece)]

    def w_block(owner):
        return w_all.at[pl.ds(pl.multiple_of(owner * depth, 16), depth)]

    def o_rows(owner, kind, part):
        return o_all.at[owner, kind, pl.ds(pl.multiple_of(part * o_half, 16), o_half)]

    loads = [pltpu.make_async_copy(a, b, local.at[k]) for k, (a, b) in enumerate(((hidden, n_all.at[place]), (wq, w_block(tile))))]
    load_o = pltpu.make_async_copy(wo, o_all.at[tile, 0], local.at[2])
    for way in (0, 1):
        start(lambda way=way: goes_on(place, seqs, way), lambda way=way: (hidden, n_all.at[place], nz_s.at[way, 1], nz_r.at[way, 1], along(way)))
    for at in range(chunks):
        start(yes, lambda at=at: (
            wq.at[pl.ds(pl.multiple_of(group * q_half + at * piece, 16), piece)], w_rows(tile, group, at),
            qx_s.at[at], qx_r.at[at], x_dev))
    for load in loads:
        load.start()
    start(yes, lambda: (wq, w_block(tile), qo_s, qo_r, p_dev))
    start(middle, lambda: (wo, o_all.at[tile, 0], ox_s.at[0], ox_r.at[0], x_dev))
    run(inner, load_o.start)
    start(middle, lambda: (wo, o_all.at[tile, 0], oc_s.at[0, 0], oc_r.at[0, 0], p_dev))

    values[:, :, HD:] = jnp.ones((heads, values.shape[1], HD), values.dtype)

    def tokens(far):
        for way in (0, 1):
            here = arrives(place, seqs, way, far)
            row = functools.partial(lambda way: place - far if way == 0 else place + far, way)
            arrived(here, lambda row=row: n_all.at[row()], nz_r.at[way, far])
            if far < seqs - 1:
                start(
                    lambda way=way: both(arrives(place, seqs, way, far), goes_on(place, seqs, way)),
                    lambda row=row, way=way: (
                        n_all.at[row()], n_all.at[row()], nz_s.at[way, far + 1], nz_r.at[way, far + 1], along(way)))

    def q_over(at):
        arrived(None, lambda: w_rows(over, group, at), qx_r.at[at])
        start(yes, lambda: (w_rows(over, group, at), w_rows(over, group, at), qy_s.at[at], qy_r.at[at], y_dev))
        start(yes, lambda: (w_rows(over, group, at), w_rows(over, group, at), qc_s.at[0, at], qc_r.at[group, at], p_dev))

    def q_peer(at):
        arrived(None, lambda: w_rows(over, 1 - group, at), qy_r.at[at])
        start(yes, lambda: (
            w_rows(over, 1 - group, at), w_rows(over, 1 - group, at), qc_s.at[1, at], qc_r.at[1 - group, at], p_dev))

    def o_first():
        start(ends, lambda: (
            wo.at[pl.ds(pl.multiple_of(group * o_half, 16), o_half)], o_rows(tile, 2, group), oz_s.at[0], oz_r.at[2], in_dev))
        start(middle, lambda: (
            wo.at[pl.ds(pl.multiple_of(group * o_half, 16), o_half)], o_rows(tile, 1, group), oz_s.at[1], oz_r.at[1], in_dev))

    def o_chain(kind):
        arrived(inner, lambda: o_rows(tile, kind, group), oz_r.at[kind])
        if kind == 2:
            start(middle, lambda: (o_rows(tile, 2, group), o_rows(tile, 3, group), oz_s.at[2], oz_r.at[3], in_dev))
        start(middle, lambda: (o_rows(tile, kind, group), o_rows(tile, kind, group), ox_s.at[kind], ox_r.at[kind], x_dev))
        start(middle, lambda: (o_rows(tile, kind, group), o_rows(tile, kind, group), oy_s.at[0, kind], oy_r.at[0, kind], y_dev))

    def o_over(kind):
        if kind == 0:
            arrived(inner, lambda: o_all.at[over, 0], ox_r.at[0])
            start(middle, lambda: (o_all.at[over, 0], o_all.at[over, 0], oc_s.at[1, 0], oc_r.at[1, 0], p_dev))
        else:
            arrived(inner, lambda: o_rows(over, kind, group), ox_r.at[kind])
            start(middle, lambda: (
                o_rows(over, kind, group), o_rows(over, kind, group), oy_s.at[1, kind], oy_r.at[1, kind], y_dev))

    def o_peer(which, kind):
        owner = tile if which == 0 else over
        arrived(inner, lambda: o_rows(owner, kind, 1 - group), oy_r.at[which, kind])
        start(middle, lambda: (
            o_all.at[owner, kind], o_all.at[owner, kind], oc_s.at[which, kind], oc_r.at[which, kind], p_dev))

    q_over(0)
    for at in range(1, chunks):
        if at == chunks - 1:
            tokens(1)
            o_first()
        q_over(at)
        q_peer(at - 1)
    q_peer(chunks - 1)
    for load in loads:
        load.wait()
    arrived(None, lambda: w_block(mate), qo_r)
    for part in (0, 1):
        for at in range(chunks):
            arrived(None, lambda: w_rows(mate_over, part, at), qc_r.at[part, at])

    strip = 32

    def project(row):
        def norm(at, carry):
            rows = pl.ds(pl.multiple_of(at * strip, strip), strip)
            given = n_all[row, rows, :].astype(jnp.float32)
            normed[rows, :] = (layer_norm(given) * (1.0 + modulation[1:2]) + modulation[0:1]).astype(normed.dtype)
            return carry

        lax.fori_loop(0, block // strip, norm, 0)
        place_of = pl.ds(pl.multiple_of(row * block, block), block)

        def one(pair, carry):
            part = jnp.dot(
                normed[...], w_all[:, pl.ds(pl.multiple_of(pair * (6 * HD), 128), 6 * HD)], preferred_element_type=jnp.float32
            )
            for at in (0, 1):
                here = 3 * HD * at
                queries[2 * pair + at, place_of, :] = root_norm(part[:, here : here + HD]).astype(queries.dtype)
                keys[2 * pair + at, place_of, :] = root_norm(part[:, here + HD : here + 2 * HD]).astype(keys.dtype)
                values[2 * pair + at, place_of, pl.ds(0, HD)] = part[:, here + 2 * HD : here + 3 * HD].astype(values.dtype)
            return carry

        lax.fori_loop(0, pairs, one, 0)

    def in_order(step, carry):
        @pl.when(step == 1)
        def _():
            o_chain(2)

        @pl.when(step == 3)
        def _():
            tokens(2)

        @pl.when(step == 5)
        def _():
            o_over(0)
            o_peer(0, 2)
            o_over(2)
            o_chain(1)
            tokens(3)

        far, way = (step + 1) // 2, (step + 1) % 2
        row = place + far * (2 * way - 1)

        @pl.when(both(row >= 0, row < seqs))
        def _():
            project(row)

        return carry

    lax.fori_loop(0, 2 * seqs - 1, in_order, 0)

    def slot_of(row):
        return row // 2 + 1, 0 if row in (1, 2) else 1

    def kind_at(target):
        return 2 * outer_end.astype(jnp.int32) + (side != target // 2).astype(jnp.int32)

    def leave(pair, row):
        target, slot = slot_of(row)
        kind = kind_at(target)
        source = attended.at[pair, pl.ds(row * block, block)]
        landing = att_in.at[kind, pair, pl.ds(slot * block, block)]
        away = copy(source, landing, at_s.at[row, pair], at_r.at[kind, slot, pair], {"seq": target})
        stay = pltpu.make_async_copy(source, landing, at_r.at[kind, slot, pair])
        return place != target, away, place == target, stay

    def one_head(head, carry):
        pair = head // 2
        lanes = pl.ds(pl.multiple_of((head % 2) * HD, HD), HD)
        for row in range(seqs):
            at = pl.ds(row * block, block)
            scores = lax.dot_general(
                queries[head, at, :], keys[head], (((1,), (1,)), ((), ())), preferred_element_type=jnp.float32
            )
            expo = jnp.exp2(scores * scale).astype(jnp.bfloat16)
            mixed = jnp.dot(expo, values[head], preferred_element_type=jnp.float32)
            attended[pair, at, lanes] = (mixed[:, :HD] * (1.0 / mixed[:, HD:])).astype(attended.dtype)

        @pl.when(head % 2 == 1)
        def _():
            for row in range(seqs):
                far, away, near, stay = leave(pair, row)
                run(far, away.start)
                run(near, stay.start)

        @pl.when(head == 1)
        def _():
            o_peer(1, 2)

        @pl.when(head == heads // 2)
        def _():
            o_chain(3)
            o_over(1)

        @pl.when(head == heads - 1)
        def _():
            o_peer(0, 1)
            o_over(3)

        return carry

    lax.fori_loop(0, heads, one_head, 0)

    @pl.when(inner)
    def _():
        summed[...] = jnp.zeros_like(summed)

    run(inner, load_o.wait)

    def accumulate(kind, carry):
        @pl.when(kind == 1)
        def _():
            o_peer(1, 1)

        @pl.when(kind == 3)
        def _():
            o_peer(0, 3)
            o_peer(1, 3)

        @pl.when(inner)
        def _():
            copy(o_all.at[mate, kind], o_all.at[mate, kind], oc_s.at[0, kind], oc_r.at[0, kind], p_dev).wait_recv()
            copy(o_all.at[mate_over, kind], o_all.at[mate_over, kind], oc_s.at[1, kind], oc_r.at[1, kind], p_dev).wait_recv()

            for slot in (0, 1):
                for pair in range(pairs):
                    landing = att_in.at[kind, pair, pl.ds(slot * block, block)]
                    source = attended.at[pair, pl.ds(0, block)]
                    got = at_r.at[kind, slot, pair]

                    @pl.when(kind == 0)
                    def _():
                        pltpu.make_async_copy(source, landing, got).wait()

                    @pl.when(kind != 0)
                    def _():
                        copy(landing, landing, got, got, p_dev).wait_recv()

            def columns(owner, carry):
                here = pl.ds(pl.multiple_of(owner * wo.shape[1], 128), wo.shape[1])
                total = summed[:, here]
                for pair in range(pairs):
                    total += jnp.dot(
                        att_in[kind, pair], o_all[owner, kind, pl.ds(pair * 2 * HD, 2 * HD), :],
                        preferred_element_type=jnp.float32,
                    )
                summed[:, here] = total
                return carry

            lax.fori_loop(0, o_all.shape[0], columns, 0)

        return carry

    lax.fori_loop(0, seqs, accumulate, 0)

    def send_vel():
        return copy(vel.at[1], vel_in, vl_s, vl_r, out_dev)

    @pl.when(inner)
    def _():
        def finish(step, carry):
            slot = 1 - step
            row = place - toward * slot

            def norm(at, carry):
                rows = pl.ds(pl.multiple_of(at * strip, strip), strip)
                sums = pl.ds(pl.multiple_of(slot * block + at * strip, strip), strip)
                mixed = n_all[row, rows, :].astype(jnp.float32) + modulation[2:3] * summed[sums, :]
                normed[rows, :] = (layer_norm(mixed) * (1.0 + modulation[4:5]) + modulation[3:4]).astype(normed.dtype)
                return carry

            lax.fori_loop(0, block // strip, norm, 0)
            vel[slot] = lax.dot_general(
                w_head[...], normed[...], (((1,), (1,)), ((), ())), preferred_element_type=jnp.float32
            )

            @pl.when(slot == 1)
            def _():
                send_vel().start()

            return carry

        lax.fori_loop(0, 2, finish, 0)
        velocity[...] = vel[0]
        send_vel().wait_send()

    @pl.when(outer_end)
    def _():
        copy(vel_in, vel_in, vl_s, vl_r, p_dev).wait_recv()
        velocity[...] = vel_in[...]

    def drain(pair, carry):
        for row in range(seqs):
            far, away, _, _ = leave(pair, row)
            run(far, away.wait_send)
        return carry

    lax.fori_loop(0, pairs, drain, 0)
    for cond, make in sent:
        run(cond(), lambda make=make: copy(*make()).wait_send())


def fused(hidden, wq, wo, modulation, w_head):
    tiles, seqs = lax.axis_size("tile"), lax.axis_size("seq")
    block, width = hidden.shape
    length, heads = seqs * block, wq.shape[1] // (3 * HD)
    pairs, chunks = heads // 2, 3
    sizes = [(2, seqs)] * 2 + [(chunks,)] * 4 + [(2, chunks)] * 2 + [()] * 2 + [(3,), (4,)] + [(4,)] * 2 + [(2, 4)] * 4
    sizes += [(seqs, pairs), (4, 2, pairs), (), ()]
    any_space, vmem = pl.BlockSpec(memory_space=pl.ANY), pl.BlockSpec(memory_space=pltpu.VMEM)
    return pl.pallas_call(
        functools.partial(step_kernel, math.log2(math.e) / math.sqrt(HD)),
        out_shape=jax.ShapeDtypeStruct((w_head.shape[0], block), jnp.float32),
        in_specs=[any_space] * 3 + [vmem] * 2,
        out_specs=vmem,
        scratch_shapes=[
            pltpu.VMEM((seqs, block, width), hidden.dtype),
            pltpu.VMEM((block, width), hidden.dtype),
            pltpu.VMEM((tiles * wq.shape[0], wq.shape[1]), wq.dtype),
            pltpu.VMEM((heads, length, HD), hidden.dtype),
            pltpu.VMEM((heads, length, HD), hidden.dtype),
            pltpu.VMEM((heads, length, 2 * HD), hidden.dtype),
            pltpu.VMEM((pairs, length, 2 * HD), hidden.dtype),
            pltpu.VMEM((4, pairs, 2 * block, 2 * HD), hidden.dtype),
            pltpu.VMEM((tiles, 4) + wo.shape, wo.dtype),
            pltpu.VMEM((2 * block, width), jnp.float32),
            pltpu.VMEM((2, w_head.shape[0], block), jnp.float32),
            pltpu.VMEM((w_head.shape[0], block), jnp.float32),
            pltpu.SemaphoreType.DMA((3,)),
        ]
        + [pltpu.SemaphoreType.DMA(shape) for shape in sizes],
        compiler_params=pltpu.CompilerParams(collective_id=1, has_side_effects=True, vmem_limit_bytes=67043328),
    )(hidden, wq, wo, modulation, w_head)


def fits(hidden, w_qkv, w_out):
    sizes = tuple(lax.axis_size(name) for name in ("group", "tile", "seq"))
    heads = w_qkv.shape[1] // (3 * HD)
    return sizes == (2, 4, 4) and heads % 2 == 0 and w_out.shape[1] % 128 == 0 and w_qkv.shape[0] % 96 == 0


def spread(hidden, modulation, w_qkv, w_out, w_head):
    local = hidden[0].astype(jnp.float32)
    norm_in = (layer_norm(local) * (1.0 + modulation[1]) + modulation[0]).astype(jnp.bfloat16)
    _, out_blocks, attended = gather(norm_in, w_qkv, w_out)
    attended = lax.all_to_all(attended, "seq", split_axis=0, concat_axis=1, tiled=True)
    out_blocks = out_blocks.reshape(out_blocks.shape[0], -1, out_blocks.shape[3])
    return tail(attended, out_blocks, hidden[0], modulation, w_head)


def shards(hidden, modulation, w_qkv, w_out, w_head, latent, weights_int, step_index):
    if fits(hidden, w_qkv, w_out):
        velocity = fused(hidden[0], w_qkv, w_out, modulation, w_head.T)
    else:
        velocity = spread(hidden, modulation, w_qkv, w_out, w_head).T
    index = step_index[0].astype(jnp.float32)
    now = noise_level(index, NSTEPS)
    after = noise_level(index + 1.0, NSTEPS)
    base = latent[0].T
    weight = weights_int[0].astype(jnp.float32)
    moved = base + (after - now) * velocity
    guess = base - now * velocity
    weighted = jnp.concatenate([moved, guess], axis=0) * weight[None, :]
    seq_count, tile_count = lax.axis_size("seq"), lax.axis_size("tile")
    jump = seq_count - 2
    moves = [
        (t * seq_count + s, (t + 1) * seq_count + s - jump)
        for t in range(tile_count - 1)
        for s in range(jump, seq_count)
    ]
    moves = moves + [(there, here) for here, there in moves]
    other_sums = lax.ppermute(weighted.astype(jnp.bfloat16), ("tile", "seq"), moves)
    other_weight = lax.ppermute(weight.astype(jnp.bfloat16), ("tile", "seq"), moves)
    totals = weighted + other_sums.astype(jnp.float32)
    norms = weight + other_weight.astype(jnp.float32)
    joined = totals / norms[None, :]
    channels = velocity.shape[0]
    return (joined[:channels].T[None], joined[channels:].T[None])


def solution(mesh):
    in_specs = (
        P(("group", "tile"), "seq", None),
        P("group", None),
        P("tile", "seq"),
        P("seq", "tile"),
        P(),
        P(("group", "tile"), "seq", None),
        P(("group", "tile"), "seq"),
        P("group"),
    )
    out_specs = (P(("group", "tile"), "seq", None), P(("group", "tile"), "seq", None))
    return jax.shard_map(shards, mesh=mesh, in_specs=in_specs, out_specs=out_specs, check_vma=False)
```

```python
import functools
import math

import jax
import jax.numpy as jnp
from jax import lax
from jax.experimental import pallas as pl
from jax.experimental.pallas import tpu as pltpu
from jax.sharding import PartitionSpec as P

HD = 128
NSTEPS = 28


def layer_norm(values):
    mean = jnp.mean(values, axis=-1, keepdims=True)
    centred = values - mean
    spread = jnp.mean(centred * centred, axis=-1, keepdims=True)
    return centred * lax.rsqrt(spread + 1e-06)


def root_norm(values):
    return values * lax.rsqrt(jnp.mean(values * values, axis=-1, keepdims=True) + 1e-06)


def noise_level(index, steps):
    level = 1.0 - index / steps
    return 3.0 * level / (1.0 + 2.0 * level)


MESH = pl.DeviceIdType.MESH


def run(cond, body):
    if cond is None:
        body()
    else:
        pl.when(cond)(body)


def arrives(place, count, way, far):
    return place >= far if way == 0 else place <= count - 1 - far


def goes_on(place, count, way):
    return place < count - 1 if way == 0 else place > 0


def gather_kernel(
    groups, chips, seqs, scale, norm, wq, wo, q_all, o_all, attended,
    n_all, v_wq, v_wo, w_head, queries, keys, values, local, w_sem,
    nz_s, nz_r, oz_s, oz_r, qx_s, qx_r, ox_s, ox_r, qy_s, qy_r, oy_s, oy_r, qc_s, qc_r, oc_s, oc_r,
):
    group, tile, place = lax.axis_index("group"), lax.axis_index("tile"), lax.axis_index("seq")
    chip, core = tile // 2, tile % 2
    other = 1 - core
    partner = {"tile": chip * 2 + other}
    q_rows, o_rows = wq.shape[0] // groups, wo.shape[0] // groups
    both = jnp.logical_and

    def q_part(owner, part):
        return q_all.at[owner, pl.ds(pl.multiple_of(part * q_rows, 8), q_rows)]

    def o_part(owner, row, part):
        return o_all.at[owner, row, pl.ds(pl.multiple_of(part * o_rows, 8), o_rows)]

    def along_seq(way):
        return {"seq": place + 1 - 2 * way}

    def along_chip(way):
        return {"tile": tile + 2 - 4 * way}

    def peer(step):
        return {"group": (group + step) % groups}

    barrier = pltpu.get_barrier_semaphore()
    greet = [(goes_on(place, seqs, way), along_seq(way)) for way in (0, 1)]
    greet += [(goes_on(chip, chips, way), along_chip(way)) for way in (0, 1)]
    greet += [(None, peer(step)) for step in range(1, groups)] + [(None, partner)]
    for cond, device in greet:
        run(cond, lambda device=device: pl.semaphore_signal(barrier, inc=1, device_id=device, device_id_type=MESH))
    met = groups + sum(goes_on(at, count, way).astype(jnp.int32) for at, count in ((place, seqs), (chip, chips)) for way in (0, 1))
    pl.semaphore_wait(barrier, met)

    sent = []

    def copy(source, target, send, recv, device):
        return pltpu.make_async_remote_copy(
            src_ref=source, dst_ref=target, send_sem=send, recv_sem=recv, device_id=device, device_id_type=MESH
        )

    def start(cond, *made):
        run(cond, lambda: copy(*made).start())
        sent.append((cond, made))

    def arrived(cond, target, send, recv, device):
        run(cond, lambda: copy(target, target, send, recv, device).wait_recv())

    def q_to_peers(cond, at, source):
        for step in range(1, groups):
            start(cond, source, q_part(at * 2 + core, group), qy_s.at[at, step], qy_r.at[at, step], peer(step))

    def q_to_partner(cond, at, part, source):
        start(cond, source, q_part(at * 2 + core, part), qc_s.at[at, part], qc_r.at[at, part], partner)

    def o_to_peers(cond, at, row, source):
        for step in range(1, groups):
            start(cond, source, o_part(at * 2 + core, row, group), oy_s.at[at, row, step], oy_r.at[at, row, step], peer(step))

    def o_to_partner(cond, at, row, part, source):
        start(cond, source, o_part(at * 2 + core, row, part), oc_s.at[at, row, part], oc_r.at[at, row, part], partner)

    def o_along_chip(cond, way, far, at, row, source):
        start(cond, source, o_part(at * 2 + core, row, group), ox_s.at[way, far, row], ox_r.at[way, far, row], along_chip(way))

    loads = [pltpu.make_async_copy(a, b, local.at[k]) for k, (a, b) in enumerate(((norm, n_all.at[place]), (wq, v_wq), (wo, v_wo)))]
    for load in loads:
        load.start()

    own_q = wq.at[pl.ds(pl.multiple_of(group * q_rows, 8), q_rows)]
    own_o = wo.at[pl.ds(pl.multiple_of(group * o_rows, 8), o_rows)]
    for way in (0, 1):
        go = goes_on(place, seqs, way)
        start(go, norm, n_all.at[place], nz_s.at[way, 1], nz_r.at[way, 1], along_seq(way))
        start(go, own_o, o_part(tile, place, group), oz_s.at[way, 1], oz_r.at[way, 1], along_seq(way))
        go = goes_on(chip, chips, way)
        start(go, own_q, q_part(tile, group), qx_s.at[way, 1], qx_r.at[way, 1], along_chip(way))
        o_along_chip(go, way, 1, chip, place, own_o)
    for part in range(groups):
        q_to_partner(None, chip, part, wq.at[pl.ds(part * q_rows, q_rows)])
        o_to_partner(None, chip, place, part, wo.at[pl.ds(part * o_rows, o_rows)])

    stores = [pltpu.make_async_copy(b, a, local.at[k]) for k, (a, b) in enumerate(((q_all.at[tile], v_wq), (o_all.at[tile, place], v_wo)))]
    for load in loads:
        load.wait()
    for store in stores:
        store.start()

    def rows_from_chips(rows):
        for far in range(1, chips):
            for way in (0, 1):
                at = chip - far if way == 0 else chip + far
                for given, row in rows:
                    here = arrives(chip, chips, way, far)
                    here = here if given is None else both(here, given)
                    piece = o_part(at * 2 + core, row, group)
                    arrived(here, piece, ox_s.at[way, far, row], ox_r.at[way, far, row], along_chip(way))
                    if far < chips - 1:
                        o_along_chip(both(here, goes_on(chip, chips, way)), way, far + 1, at, row, piece)
                    o_to_peers(here, at, row, piece)
                    o_to_partner(here, at, row, group, piece)

    def rows_at(far):
        if far == 0:
            return [(None, place)]
        return [(arrives(place, seqs, way, far), place - far if way == 0 else place + far) for way in (0, 1)]

    def out_step(far):
        for way in (0, 1):
            here = arrives(place, seqs, way, far)
            row = place - far if way == 0 else place + far
            piece = o_part(tile, row, group)
            arrived(here, piece, oz_s.at[way, far], oz_r.at[way, far], along_seq(way))
            if far < seqs - 1:
                start(both(here, goes_on(place, seqs, way)), piece, piece, oz_s.at[way, far + 1], oz_r.at[way, far + 1], along_seq(way))
            for side in (0, 1):
                o_along_chip(both(here, goes_on(chip, chips, side)), side, 1, chip, row, piece)
            o_to_peers(here, chip, row, piece)
            o_to_partner(here, chip, row, group, piece)

    def norm_step(far):
        for way in (0, 1):
            here = arrives(place, seqs, way, far)
            row = place - far if way == 0 else place + far
            piece = n_all.at[row]
            arrived(here, piece, nz_s.at[way, far], nz_r.at[way, far], along_seq(way))
            if far < seqs - 1:
                start(both(here, goes_on(place, seqs, way)), piece, piece, nz_s.at[way, far + 1], nz_r.at[way, far + 1], along_seq(way))

    def chip_step(far):
        for way in (0, 1):
            here = arrives(chip, chips, way, far)
            at = chip - far if way == 0 else chip + far
            piece = q_part(at * 2 + core, group)
            arrived(here, piece, qx_s.at[way, far], qx_r.at[way, far], along_chip(way))
            if far < chips - 1:
                start(both(here, goes_on(chip, chips, way)), piece, piece, qx_s.at[way, far + 1], qx_r.at[way, far + 1], along_chip(way))
            q_to_peers(here, at, piece)
            q_to_partner(here, at, group, piece)

    def q_from_peers():
        for step in range(1, groups):
            part = (group + groups - step) % groups
            for at in range(chips):
                away = chip != at
                piece = q_part(at * 2 + core, part)
                arrived(away, piece, qy_s.at[at, step], qy_r.at[at, step], partner)
                q_to_partner(away, at, part, piece)

    def o_from_peers():
        for step in range(1, groups):
            part = (group + groups - step) % groups
            for at in range(chips):
                for row in range(seqs):
                    away = jnp.logical_or(chip != at, place != row)
                    piece = o_part(at * 2 + core, row, part)
                    arrived(away, piece, oy_s.at[at, row, step], oy_r.at[at, row, step], partner)
                    o_to_partner(away, at, row, part, piece)

    last = max(chips, seqs) - 1
    for far in range(1, last + 1):
        if 1 < far < seqs:
            rows_from_chips(rows_at(far - 1))
        if far < seqs:
            norm_step(far)
        if far < seqs - 1:
            out_step(far)
        if far < chips:
            chip_step(far)
        if far == 1 and seqs > 1:
            rows_from_chips(rows_at(0))
        if far == max(chips - 1, min(2, last)):
            q_from_peers()
    for at in range(chips):
        for part in range(groups):
            arrived(None, q_part(at * 2 + other, part), qc_s.at[at, part], qc_r.at[at, part], partner)
    for store in stores:
        store.wait()

    heads = wq.shape[1] // (3 * HD)
    depth, block = wq.shape[0], norm.shape[0]

    def fetch(head):
        slot = head % 2
        columns = pl.ds(pl.multiple_of(head * (3 * HD), 128), 3 * HD)
        return [
            pltpu.make_async_copy(
                q_all.at[at, :, columns], w_head.at[slot, pl.ds(at * depth, depth)], w_sem.at[slot, at]
            )
            for at in range(2 * chips)
        ]

    def one_head(head, carry):
        for load in fetch(head):
            load.wait()

        @pl.when(head + 1 < heads)
        def _():
            for load in fetch(head + 1):
                load.start()

        weights = w_head.at[head % 2]
        for row in range(seqs):
            at = pl.ds(row * block, block)
            part = jnp.dot(n_all[row], weights[...], preferred_element_type=jnp.float32)
            queries[at, :] = root_norm(part[:, :HD]).astype(jnp.bfloat16)
            keys[at, :] = root_norm(part[:, HD : 2 * HD]).astype(jnp.bfloat16)
            values[at, :] = part[:, 2 * HD :].astype(jnp.bfloat16)
        for row in range(seqs):
            at = pl.ds(row * block, block)
            scores = lax.dot_general(
                queries[at, :], keys[...], (((1,), (1,)), ((), ())), preferred_element_type=jnp.float32
            )
            expo = jnp.exp(scores * scale)
            probs = (expo * (1.0 / jnp.sum(expo, axis=-1, keepdims=True))).astype(jnp.bfloat16)
            attended[at, pl.ds(pl.multiple_of(head * HD, 128), HD)] = jnp.dot(
                probs, values[...], preferred_element_type=jnp.float32
            ).astype(jnp.bfloat16)
        return carry

    def between(step):
        if step == 0 and seqs > 1:
            out_step(seqs - 1)
        if step == 1:
            rows_from_chips(rows_at(seqs - 1))
        if step == 2:
            o_from_peers()

    for load in fetch(0):
        load.start()
    cuts = [0, heads // 3, heads // 2, 5 * heads // 6, heads]
    for step in range(4):
        if cuts[step] < cuts[step + 1]:
            lax.fori_loop(cuts[step], cuts[step + 1], one_head, 0)
        between(step)

    for at in range(chips):
        for part in range(groups):
            for row in range(seqs):
                arrived(None, o_part(at * 2 + other, row, part), oc_s.at[at, row, part], oc_r.at[at, row, part], partner)
    for cond, made in sent:
        run(cond, lambda made=made: copy(*made).wait_send())


def gather(norm, wq, wo):
    groups, tiles, seqs = (lax.axis_size(name) for name in ("group", "tile", "seq"))
    chips = tiles // 2
    length = seqs * norm.shape[0]
    pairs = [(2, seqs), (2, seqs), (2, chips), (2, chips, seqs), (chips, groups), (chips, seqs, groups), (chips, groups), (chips, seqs, groups)]
    return pl.pallas_call(
        functools.partial(gather_kernel, groups, chips, seqs, 1.0 / math.sqrt(HD)),
        out_shape=(
            jax.ShapeDtypeStruct((tiles,) + wq.shape, wq.dtype),
            jax.ShapeDtypeStruct((tiles, seqs) + wo.shape, wo.dtype),
            jax.ShapeDtypeStruct((length, wq.shape[1] // 3), norm.dtype),
        ),
        in_specs=[pl.BlockSpec(memory_space=pl.ANY)] * 3,
        out_specs=(pl.BlockSpec(memory_space=pl.ANY),) * 2 + (pl.BlockSpec(memory_space=pltpu.VMEM),),
        scratch_shapes=[pltpu.VMEM((seqs,) + norm.shape, norm.dtype)]
        + [pltpu.VMEM(a.shape, a.dtype) for a in (wq, wo)]
        + [pltpu.VMEM((2, tiles * wq.shape[0], 3 * HD), wq.dtype)]
        + [pltpu.VMEM((length, HD), norm.dtype)] * 3
        + [pltpu.SemaphoreType.DMA((3,)), pltpu.SemaphoreType.DMA((2, tiles))]
        + [pltpu.SemaphoreType.DMA(shape) for shape in pairs for _ in range(2)],
        compiler_params=pltpu.CompilerParams(collective_id=0, has_side_effects=True),
    )(norm, wq, wo)


def tail_kernel(attended, blocks, hidden, modulation, w_head, velocity, summed):
    at = pl.program_id(0)
    width = blocks.shape[2]
    here = pl.ds(pl.multiple_of(at * width, 128), width)
    summed[:, here] = jnp.dot(attended[...], blocks[0], preferred_element_type=jnp.float32)

    @pl.when(at == pl.num_programs(0) - 1)
    def _():
        mixed = hidden[...].astype(jnp.float32) + modulation[2:3] * summed[...]
        norm_out = (layer_norm(mixed) * (1.0 + modulation[4:5]) + modulation[3:4]).astype(jnp.bfloat16)
        velocity[...] = jnp.dot(norm_out, w_head[...], preferred_element_type=jnp.float32)


def tail(attended, blocks, hidden, modulation, w_head):
    tiles, depth, width = blocks.shape
    if width % 128:
        summed = jnp.concatenate(
            [jnp.dot(attended, blocks[at], preferred_element_type=jnp.float32) for at in range(tiles)], axis=1
        )
        mixed = hidden.astype(jnp.float32) + modulation[2] * summed
        norm_out = (layer_norm(mixed) * (1.0 + modulation[4]) + modulation[3]).astype(jnp.bfloat16)
        return jnp.dot(norm_out, w_head, preferred_element_type=jnp.float32)
    whole = [pl.BlockSpec(a.shape, lambda at: (0, 0), pipeline_mode=pl.Buffered(1)) for a in (attended, hidden, modulation, w_head)]
    return pl.pallas_call(
        tail_kernel,
        grid=(tiles,),
        out_shape=jax.ShapeDtypeStruct((hidden.shape[0], w_head.shape[1]), jnp.float32),
        in_specs=[whole[0], pl.BlockSpec((1, depth, width), lambda at: (at, 0, 0)), *whole[1:]],
        out_specs=pl.BlockSpec((hidden.shape[0], w_head.shape[1]), lambda at: (0, 0)),
        scratch_shapes=[pltpu.VMEM(hidden.shape, jnp.float32)],
    )(attended, blocks, hidden, modulation, w_head)


def step_kernel(
    scale, hidden, wq, wo, modulation, w_head, latent, weight, index, stepped, clean,
    n_all, normed, w_all, queries, keys, values, attended, att_in, o_all, summed,
    lat_in, wt_in, joint, msg, msg_in, result, local,
    nz_s, nz_r, qx_s, qx_r, qy_s, qy_r, qc_s, qc_r, qo_s, qo_r, oz_s, oz_r, ox_s, ox_r, oy_s, oy_r, oc_s, oc_r,
    at_s, at_r, ln_s, ln_r, wt_s, wt_r, ms_s, ms_r, rs_s, rs_r,
):
    group, tile, place = lax.axis_index("group"), lax.axis_index("tile"), lax.axis_index("seq")
    seqs, block, width = n_all.shape
    chip, core = tile // 2, tile % 2
    side = place // 2
    toward = 1 - 2 * side
    inner = jnp.logical_or(place == 1, place == 2)
    outer_end = jnp.logical_not(inner)
    over = (1 - chip) * 2 + core
    mate = chip * 2 + 1 - core
    mate_over = (1 - chip) * 2 + 1 - core
    x_dev, y_dev, p_dev, in_dev = {"tile": over}, {"group": 1 - group}, {"tile": mate}, {"seq": place + toward}
    out_dev = {"seq": place - toward}
    depth, cols = wq.shape
    q_half, o_half = depth // 2, wo.shape[0] // 2
    chunks = qx_s.shape[0]
    piece = q_half // chunks
    pairs = attended.shape[0]
    heads = queries.shape[0]
    both = jnp.logical_and

    def yes():
        return None

    def middle():
        return inner

    def ends():
        return outer_end

    def along(way):
        return {"seq": place + 1 - 2 * way}

    barrier = pltpu.get_barrier_semaphore()
    greet = [x_dev, y_dev, p_dev] + [{"seq": (place + far) % seqs} for far in range(1, seqs)]
    for device in greet:
        pl.semaphore_signal(barrier, inc=1, device_id=device, device_id_type=MESH)
    step_tile = 2 * side - 1
    tiles = lax.axis_size("tile")
    paired = jnp.logical_and(inner, jnp.logical_and(tile + step_tile >= 0, tile + step_tile < tiles))
    j_dev = {"tile": tile + step_tile, "seq": seqs - 1 - place}

    @pl.when(paired)
    def _():
        pl.semaphore_signal(barrier, inc=1, device_id=j_dev, device_id_type=MESH)

    pl.semaphore_wait(barrier, len(greet) + paired.astype(jnp.int32))

    sent = []

    def copy(source, target, send, recv, device):
        return pltpu.make_async_remote_copy(
            src_ref=source, dst_ref=target, send_sem=send, recv_sem=recv, device_id=device, device_id_type=MESH
        )

    def start(cond, make):
        run(cond(), lambda: copy(*make()).start())
        sent.append((cond, make))

    def arrived(cond, target, recv):
        run(cond, lambda: copy(target(), target(), recv, recv, p_dev).wait_recv())

    def w_rows(owner, part, at):
        return w_all.at[pl.ds(pl.multiple_of(owner * depth + part * q_half + at * piece, 16), piece)]

    def w_block(owner):
        return w_all.at[pl.ds(pl.multiple_of(owner * depth, 16), depth)]

    def o_rows(owner, kind, part):
        return o_all.at[owner, kind, pl.ds(pl.multiple_of(part * o_half, 16), o_half)]

    loads = [pltpu.make_async_copy(a, b, local.at[k]) for k, (a, b) in enumerate(((hidden, n_all.at[place]), (wq, w_block(tile))))]
    load_o = pltpu.make_async_copy(wo, o_all.at[tile, 0], local.at[2])
    for way in (0, 1):
        start(lambda way=way: goes_on(place, seqs, way), lambda way=way: (hidden, n_all.at[place], nz_s.at[way, 1], nz_r.at[way, 1], along(way)))
    for at in range(chunks):
        start(yes, lambda at=at: (
            wq.at[pl.ds(pl.multiple_of(group * q_half + at * piece, 16), piece)], w_rows(tile, group, at),
            qx_s.at[at], qx_r.at[at], x_dev))
    for load in loads:
        load.start()
    start(yes, lambda: (wq, w_block(tile), qo_s, qo_r, p_dev))
    start(middle, lambda: (wo, o_all.at[tile, 0], ox_s.at[0], ox_r.at[0], x_dev))
    start(ends, lambda: (wo, o_all.at[tile, 2], ox_s.at[2], ox_r.at[2], x_dev))
    start(ends, lambda: (wo, o_all.at[tile, 2], oz_s.at[0], oz_r.at[2], in_dev))
    start(ends, lambda: (latent, lat_in, ln_s, ln_r, in_dev))
    start(ends, lambda: (weight, wt_in, wt_s, wt_r, in_dev))
    run(inner, load_o.start)
    start(middle, lambda: (wo, o_all.at[tile, 0], oc_s.at[0, 0], oc_r.at[0, 0], p_dev))

    values[:, :, HD:] = jnp.ones((heads, values.shape[1], HD), values.dtype)

    def tokens(far):
        for way in (0, 1):
            here = arrives(place, seqs, way, far)
            row = functools.partial(lambda way: place - far if way == 0 else place + far, way)
            arrived(here, lambda row=row: n_all.at[row()], nz_r.at[way, far])
            if far < seqs - 1:
                start(
                    lambda way=way: both(arrives(place, seqs, way, far), goes_on(place, seqs, way)),
                    lambda row=row, way=way: (
                        n_all.at[row()], n_all.at[row()], nz_s.at[way, far + 1], nz_r.at[way, far + 1], along(way)))

    def q_over(at):
        arrived(None, lambda: w_rows(over, group, at), qx_r.at[at])
        start(yes, lambda: (w_rows(over, group, at), w_rows(over, group, at), qy_s.at[at], qy_r.at[at], y_dev))
        start(yes, lambda: (w_rows(over, group, at), w_rows(over, group, at), qc_s.at[0, at], qc_r.at[group, at], p_dev))

    def q_peer(at):
        arrived(None, lambda: w_rows(over, 1 - group, at), qy_r.at[at])
        start(yes, lambda: (
            w_rows(over, 1 - group, at), w_rows(over, 1 - group, at), qc_s.at[1, at], qc_r.at[1 - group, at], p_dev))

    def o_first():
        start(middle, lambda: (
            wo.at[pl.ds(pl.multiple_of(group * o_half, 16), o_half)], o_rows(tile, 1, group), oz_s.at[1], oz_r.at[1], in_dev))

    def o_end():
        arrived(outer_end, lambda: o_all.at[over, 2], ox_r.at[2])
        start(ends, lambda: (o_all.at[over, 2], o_all.at[over, 2], oz_s.at[3], oz_r.at[0], in_dev))
        arrived(inner, lambda: o_all.at[tile, 2], oz_r.at[2])
        start(middle, lambda: (o_rows(tile, 2, group), o_rows(tile, 3, group), oz_s.at[2], oz_r.at[3], in_dev))
        start(middle, lambda: (o_all.at[tile, 2], o_all.at[tile, 2], oc_s.at[0, 2], oc_r.at[0, 2], p_dev))

    def o_end_over():
        arrived(inner, lambda: o_all.at[over, 2], oz_r.at[0])
        start(middle, lambda: (o_all.at[over, 2], o_all.at[over, 2], oc_s.at[1, 2], oc_r.at[1, 2], p_dev))

    def o_chain(kind):
        arrived(inner, lambda: o_rows(tile, kind, group), oz_r.at[kind])
        start(middle, lambda: (o_rows(tile, kind, group), o_rows(tile, kind, group), ox_s.at[kind], ox_r.at[kind], x_dev))
        start(middle, lambda: (o_rows(tile, kind, group), o_rows(tile, kind, group), oy_s.at[0, kind], oy_r.at[0, kind], y_dev))

    def o_over(kind):
        if kind == 0:
            arrived(inner, lambda: o_all.at[over, 0], ox_r.at[0])
            start(middle, lambda: (o_all.at[over, 0], o_all.at[over, 0], oc_s.at[1, 0], oc_r.at[1, 0], p_dev))
        else:
            arrived(inner, lambda: o_rows(over, kind, group), ox_r.at[kind])
            start(middle, lambda: (
                o_rows(over, kind, group), o_rows(over, kind, group), oy_s.at[1, kind], oy_r.at[1, kind], y_dev))

    def o_peer(which, kind):
        owner = tile if which == 0 else over
        arrived(inner, lambda: o_rows(owner, kind, 1 - group), oy_r.at[which, kind])
        start(middle, lambda: (
            o_all.at[owner, kind], o_all.at[owner, kind], oc_s.at[which, kind], oc_r.at[which, kind], p_dev))

    q_over(0)
    for at in range(1, chunks):
        if at == chunks - 1:
            tokens(1)
            o_first()
        q_over(at)
        q_peer(at - 1)
    q_peer(chunks - 1)
    for load in loads:
        load.wait()
    arrived(None, lambda: w_block(mate), qo_r)
    for part in (0, 1):
        for at in range(chunks):
            arrived(None, lambda: w_rows(mate_over, part, at), qc_r.at[part, at])

    strip = 32

    def norm_of(row):
        def norm(at, carry):
            rows = pl.ds(pl.multiple_of(at * strip, strip), strip)
            given = n_all[row, rows, :].astype(jnp.float32)
            normed[rows, :] = (layer_norm(given) * (1.0 + modulation[1:2]) + modulation[0:1]).astype(normed.dtype)
            return carry

        lax.fori_loop(0, block // strip, norm, 0)

    def project(row, pair):
        place_of = pl.ds(pl.multiple_of(row * block, block), block)
        part = jnp.dot(
            normed[...], w_all[:, pl.ds(pl.multiple_of(pair * (6 * HD), 128), 6 * HD)], preferred_element_type=jnp.float32
        )
        for at in (0, 1):
            here = 3 * HD * at
            queries[2 * pair + at, place_of, :] = root_norm(part[:, here : here + HD]).astype(queries.dtype)
            keys[2 * pair + at, place_of, :] = root_norm(part[:, here + HD : here + 2 * HD]).astype(keys.dtype)
            values[2 * pair + at, place_of, pl.ds(0, HD)] = part[:, here + 2 * HD : here + 3 * HD].astype(values.dtype)

    final = (seqs - 1) * (1 - side)

    def in_order(step, carry):
        @pl.when(step == 1)
        def _():
            o_end()

        @pl.when(step == 2)
        def _():
            tokens(2)

        far, way = (step + 1) // 2, (step + 1) % 2
        row = place + far * (2 * way - 1)

        @pl.when(both(both(row >= 0, row < seqs), row != final))
        def _():
            norm_of(row)
            lax.fori_loop(0, pairs, lambda pair, carry: (project(row, pair), carry)[1], 0)

        return carry

    lax.fori_loop(0, 2 * seqs - 3, in_order, 0)
    o_over(0)
    tokens(3)
    norm_of(final)

    def leave(pair, turn):
        row = (turn + 2 * (1 - side)) % seqs
        target, slot = row // 2 + 1, 1 - ((row + 1) // 2) % 2
        kind = 2 * outer_end.astype(jnp.int32) + (side != row // 2).astype(jnp.int32)
        source = attended.at[pair, pl.ds(pl.multiple_of(row * block, block), block)]
        landing = att_in.at[kind, pair, pl.ds(pl.multiple_of(slot * block, block), block)]
        got = at_r.at[kind, slot, pair]

        def away():
            return copy(source, landing, at_s.at[turn, pair], got, {"seq": target})

        def stay():
            return pltpu.make_async_copy(source, landing, got)

        return place != target, away, stay

    def one_pair(pair, carry):
        project(final, pair)
        for half in (0, 1):
            head = 2 * pair + half
            for row in range(seqs):
                at = pl.ds(row * block, block)
                scores = lax.dot_general(
                    queries[head, at, :], keys[head], (((1,), (1,)), ((), ())), preferred_element_type=jnp.float32
                )
                expo = jnp.exp2(scores * scale).astype(jnp.bfloat16)
                mixed = jnp.dot(expo, values[head], preferred_element_type=jnp.float32)
                attended[pair, at, pl.ds(half * HD, HD)] = (mixed[:, :HD] * (1.0 / mixed[:, HD:])).astype(attended.dtype)

        for turn in range(seqs):
            far, away, stay = leave(pair, turn)
            run(far, lambda away=away: away().start())
            run(jnp.logical_not(far), lambda stay=stay: stay().start())

        @pl.when(pair == 0)
        def _():
            o_chain(1)
            o_end_over()

        @pl.when(pair == pairs - 1)
        def _():
            o_chain(3)
            o_over(1)

        return carry

    lax.fori_loop(0, pairs, one_pair, 0)

    @pl.when(inner)
    def _():
        summed[...] = jnp.zeros_like(summed)

    run(inner, load_o.wait)

    def rows_here(kind):
        copy(o_all.at[mate, kind], o_all.at[mate, kind], oc_s.at[0, kind], oc_r.at[0, kind], p_dev).wait_recv()
        copy(o_all.at[mate_over, kind], o_all.at[mate_over, kind], oc_s.at[1, kind], oc_r.at[1, kind], p_dev).wait_recv()

    def attended_here(kind, slot, pair):
        landing = att_in.at[kind, pair, pl.ds(slot * block, block)]
        copy(landing, landing, at_r.at[kind, slot, pair], at_r.at[kind, slot, pair], p_dev).wait_recv()

    def add_up(kind, which):
        def columns(owner, carry):
            here = pl.ds(pl.multiple_of(owner * wo.shape[1], 128), wo.shape[1])
            total = summed[:, here]
            for pair in which:
                rows = pl.ds(pl.multiple_of(pair * 2 * HD, 2 * HD), 2 * HD)
                total += jnp.dot(att_in[kind, pair], o_all[owner, kind, rows, :], preferred_element_type=jnp.float32)
            summed[:, here] = total
            return carry

        lax.fori_loop(0, o_all.shape[0], columns, 0)

    def accumulate(kind, carry):
        @pl.when(kind == 1)
        def _():
            o_peer(0, 1)
            o_over(3)
            o_peer(1, 1)

        @pl.when(inner)
        def _():
            rows_here(kind)
            for slot in (0, 1):
                for pair in range(pairs):
                    landing = att_in.at[kind, pair, pl.ds(slot * block, block)]

                    @pl.when(kind == 0)
                    def _():
                        pltpu.make_async_copy(attended.at[pair, pl.ds(0, block)], landing, at_r.at[kind, slot, pair]).wait()

                    @pl.when(kind != 0)
                    def _():
                        attended_here(kind, slot, pair)

            add_up(kind, range(pairs))

        return carry

    lax.fori_loop(0, 2, accumulate, 0)
    o_peer(0, 3)
    o_peer(1, 3)

    def accumulate_end(at, carry):
        pair, kind = at // 2, 2 + at % 2

        @pl.when(inner)
        def _():
            @pl.when(pair == 0)
            def _():
                rows_here(kind)

            for slot in (0, 1):
                attended_here(kind, slot, pair)
            add_up(kind, [pair])

        return carry

    lax.fori_loop(0, 2 * pairs, accumulate_end, 0)

    def message(slot):
        return copy(msg.at[slot], msg_in.at[1 - slot], ms_s.at[slot], ms_r.at[1 - slot], j_dev)

    def answer():
        return copy(result, result, rs_s, rs_r, out_dev)

    channels = latent.shape[0]

    def level(offset):
        at = jnp.full((1, block), index[0], jnp.int32).astype(jnp.float32) + offset
        return noise_level(at, NSTEPS)

    @pl.when(inner)
    def _():
        copy(latent, lat_in, ln_s, ln_r, p_dev).wait_recv()
        copy(weight, wt_in, wt_s, wt_r, p_dev).wait_recv()
        now, after = level(0.0), level(1.0)
        for slot in (1, 0):
            row = place - toward * slot

            def norm(at, carry):
                rows = pl.ds(pl.multiple_of(at * strip, strip), strip)
                sums = pl.ds(pl.multiple_of(slot * block + at * strip, strip), strip)
                mixed = n_all[row, rows, :].astype(jnp.float32) + modulation[2:3] * summed[sums, :]
                normed[rows, :] = (layer_norm(mixed) * (1.0 + modulation[4:5]) + modulation[3:4]).astype(normed.dtype)
                return carry

            lax.fori_loop(0, block // strip, norm, 0)
            velocity = lax.dot_general(
                w_head[...], normed[...], (((1,), (1,)), ((), ())), preferred_element_type=jnp.float32
            )
            base = (latent if slot == 0 else lat_in)[...]
            weighs = (weight if slot == 0 else wt_in)[...].astype(jnp.float32)
            joint[slot, pl.ds(0, channels), :] = (base + (after - now) * velocity) * weighs
            joint[slot, pl.ds(channels, channels), :] = (base - now * velocity) * weighs
            msg[slot, pl.ds(0, 2 * channels), :] = joint[slot].astype(msg.dtype)
            msg[slot, pl.ds(2 * channels, 16), :] = jnp.broadcast_to(weighs, (16, block)).astype(msg.dtype)
            run(paired, lambda slot=slot: message(slot).start())

        @pl.when(jnp.logical_not(paired))
        def _():
            msg_in[...] = jnp.zeros_like(msg_in)

        for slot in (1, 0):
            run(paired, lambda slot=slot: message(1 - slot).wait_recv())
            weighs = (weight if slot == 0 else wt_in)[...].astype(jnp.float32)
            given = msg_in[slot].astype(jnp.float32)
            joined = (joint[slot] + given[: 2 * channels]) / (weighs + given[2 * channels : 2 * channels + 1])
            if slot == 1:
                joint[1] = joined
                copy(joint.at[1], result, rs_s, rs_r, out_dev).start()
            else:
                stepped[...] = joined[:channels]
                clean[...] = joined[channels:]
        for slot in (1, 0):
            run(paired, lambda slot=slot: message(slot).wait_send())
        copy(joint.at[1], result, rs_s, rs_r, out_dev).wait_send()

    @pl.when(outer_end)
    def _():
        answer().wait_recv()
        stepped[...] = result[pl.ds(0, channels), :]
        clean[...] = result[pl.ds(channels, channels), :]

    def drain(pair, carry):
        for turn in range(seqs):
            far, away, _ = leave(pair, turn)
            run(far, lambda away=away: away().wait_send())
        return carry

    lax.fori_loop(0, pairs, drain, 0)
    for cond, make in sent:
        run(cond(), lambda make=make: copy(*make()).wait_send())


def fused(hidden, wq, wo, modulation, w_head, latent, weight, index):
    tiles, seqs = lax.axis_size("tile"), lax.axis_size("seq")
    block, width = hidden.shape
    length, heads = seqs * block, wq.shape[1] // (3 * HD)
    pairs, chunks = heads // 2, 3
    channels = w_head.shape[0]
    sizes = [(2, seqs)] * 2 + [(chunks,)] * 4 + [(2, chunks)] * 2 + [()] * 2 + [(4,)] * 4 + [(2, 4)] * 4
    sizes += [(seqs, pairs), (4, 2, pairs)] + [()] * 4 + [(2,)] * 2 + [()] * 2
    any_space, vmem = pl.BlockSpec(memory_space=pl.ANY), pl.BlockSpec(memory_space=pltpu.VMEM)
    return pl.pallas_call(
        functools.partial(step_kernel, math.log2(math.e) / math.sqrt(HD)),
        out_shape=(jax.ShapeDtypeStruct((channels, block), jnp.float32),) * 2,
        in_specs=[any_space] * 3 + [vmem] * 4 + [pl.BlockSpec(memory_space=pltpu.SMEM)],
        out_specs=(vmem, vmem),
        scratch_shapes=[
            pltpu.VMEM((seqs, block, width), hidden.dtype),
            pltpu.VMEM((block, width), hidden.dtype),
            pltpu.VMEM((tiles * wq.shape[0], wq.shape[1]), wq.dtype),
            pltpu.VMEM((heads, length, HD), hidden.dtype),
            pltpu.VMEM((heads, length, HD), hidden.dtype),
            pltpu.VMEM((heads, length, 2 * HD), hidden.dtype),
            pltpu.VMEM((pairs, length, 2 * HD), hidden.dtype),
            pltpu.VMEM((4, pairs, 2 * block, 2 * HD), hidden.dtype),
            pltpu.VMEM((tiles, 4) + wo.shape, wo.dtype),
            pltpu.VMEM((2 * block, width), jnp.float32),
            pltpu.VMEM((channels, block), jnp.float32),
            pltpu.VMEM((1, block), jnp.int32),
            pltpu.VMEM((2, 2 * channels, block), jnp.float32),
            pltpu.VMEM((2, 2 * channels + 16, block), jnp.bfloat16),
            pltpu.VMEM((2, 2 * channels + 16, block), jnp.bfloat16),
            pltpu.VMEM((2 * channels, block), jnp.float32),
            pltpu.SemaphoreType.DMA((3,)),
        ]
        + [pltpu.SemaphoreType.DMA(shape) for shape in sizes],
        compiler_params=pltpu.CompilerParams(collective_id=1, has_side_effects=True, vmem_limit_bytes=67043328),
    )(hidden, wq, wo, modulation, w_head, latent, weight, index)


def fits(hidden, w_qkv, w_out):
    sizes = tuple(lax.axis_size(name) for name in ("group", "tile", "seq"))
    heads = w_qkv.shape[1] // (3 * HD)
    return sizes == (2, 4, 4) and heads % 2 == 0 and w_out.shape[1] % 128 == 0 and w_qkv.shape[0] % 96 == 0


def spread(hidden, modulation, w_qkv, w_out, w_head):
    local = hidden[0].astype(jnp.float32)
    norm_in = (layer_norm(local) * (1.0 + modulation[1]) + modulation[0]).astype(jnp.bfloat16)
    _, out_blocks, attended = gather(norm_in, w_qkv, w_out)
    attended = lax.all_to_all(attended, "seq", split_axis=0, concat_axis=1, tiled=True)
    out_blocks = out_blocks.reshape(out_blocks.shape[0], -1, out_blocks.shape[3])
    return tail(attended, out_blocks, hidden[0], modulation, w_head)


def shards(hidden, modulation, w_qkv, w_out, w_head, latent, weights_int, step_index):
    if fits(hidden, w_qkv, w_out):
        outs = fused(hidden[0], w_qkv, w_out, modulation, w_head.T, latent[0].T, weights_int, step_index)
        return tuple(out.T[None] for out in outs)
    velocity = spread(hidden, modulation, w_qkv, w_out, w_head).T
    index = step_index[0].astype(jnp.float32)
    now = noise_level(index, NSTEPS)
    after = noise_level(index + 1.0, NSTEPS)
    base = latent[0].T
    weight = weights_int[0].astype(jnp.float32)
    moved = base + (after - now) * velocity
    guess = base - now * velocity
    weighted = jnp.concatenate([moved, guess], axis=0) * weight[None, :]
    seq_count, tile_count = lax.axis_size("seq"), lax.axis_size("tile")
    jump = seq_count - 2
    moves = [
        (t * seq_count + s, (t + 1) * seq_count + s - jump)
        for t in range(tile_count - 1)
        for s in range(jump, seq_count)
    ]
    moves = moves + [(there, here) for here, there in moves]
    other_sums = lax.ppermute(weighted.astype(jnp.bfloat16), ("tile", "seq"), moves)
    other_weight = lax.ppermute(weight.astype(jnp.bfloat16), ("tile", "seq"), moves)
    totals = weighted + other_sums.astype(jnp.float32)
    norms = weight + other_weight.astype(jnp.float32)
    joined = totals / norms[None, :]
    channels = velocity.shape[0]
    return (joined[:channels].T[None], joined[channels:].T[None])


def solution(mesh):
    in_specs = (
        P(("group", "tile"), "seq", None),
        P("group", None),
        P("tile", "seq"),
        P("seq", "tile"),
        P(),
        P(("group", "tile"), "seq", None),
        P(("group", "tile"), "seq"),
        P("group"),
    )
    out_specs = (P(("group", "tile"), "seq", None), P(("group", "tile"), "seq", None))
    return jax.shard_map(shards, mesh=mesh, in_specs=in_specs, out_specs=out_specs, check_vma=False)
```

```python
import functools
import math

import jax
import jax.numpy as jnp
from jax import lax
from jax.experimental import pallas as pl
from jax.experimental.pallas import tpu as pltpu
from jax.sharding import PartitionSpec as P

HD = 128
NSTEPS = 28


def layer_norm(values):
    mean = jnp.mean(values, axis=-1, keepdims=True)
    centred = values - mean
    spread = jnp.mean(centred * centred, axis=-1, keepdims=True)
    return centred * lax.rsqrt(spread + 1e-06)


def root_norm(values):
    return values * lax.rsqrt(jnp.mean(values * values, axis=-1, keepdims=True) + 1e-06)


def noise_level(index, steps):
    level = 1.0 - index / steps
    return 3.0 * level / (1.0 + 2.0 * level)


MESH = pl.DeviceIdType.MESH


def run(cond, body):
    if cond is None:
        body()
    else:
        pl.when(cond)(body)


def arrives(place, count, way, far):
    return place >= far if way == 0 else place <= count - 1 - far


def goes_on(place, count, way):
    return place < count - 1 if way == 0 else place > 0


def gather_kernel(
    groups, chips, seqs, scale, norm, wq, wo, q_all, o_all, attended,
    n_all, v_wq, v_wo, w_head, queries, keys, values, local, w_sem,
    nz_s, nz_r, oz_s, oz_r, qx_s, qx_r, ox_s, ox_r, qy_s, qy_r, oy_s, oy_r, qc_s, qc_r, oc_s, oc_r,
):
    group, tile, place = lax.axis_index("group"), lax.axis_index("tile"), lax.axis_index("seq")
    chip, core = tile // 2, tile % 2
    other = 1 - core
    partner = {"tile": chip * 2 + other}
    q_rows, o_rows = wq.shape[0] // groups, wo.shape[0] // groups
    both = jnp.logical_and

    def q_part(owner, part):
        return q_all.at[owner, pl.ds(pl.multiple_of(part * q_rows, 8), q_rows)]

    def o_part(owner, row, part):
        return o_all.at[owner, row, pl.ds(pl.multiple_of(part * o_rows, 8), o_rows)]

    def along_seq(way):
        return {"seq": place + 1 - 2 * way}

    def along_chip(way):
        return {"tile": tile + 2 - 4 * way}

    def peer(step):
        return {"group": (group + step) % groups}

    barrier = pltpu.get_barrier_semaphore()
    greet = [(goes_on(place, seqs, way), along_seq(way)) for way in (0, 1)]
    greet += [(goes_on(chip, chips, way), along_chip(way)) for way in (0, 1)]
    greet += [(None, peer(step)) for step in range(1, groups)] + [(None, partner)]
    for cond, device in greet:
        run(cond, lambda device=device: pl.semaphore_signal(barrier, inc=1, device_id=device, device_id_type=MESH))
    met = groups + sum(goes_on(at, count, way).astype(jnp.int32) for at, count in ((place, seqs), (chip, chips)) for way in (0, 1))
    pl.semaphore_wait(barrier, met)

    sent = []

    def copy(source, target, send, recv, device):
        return pltpu.make_async_remote_copy(
            src_ref=source, dst_ref=target, send_sem=send, recv_sem=recv, device_id=device, device_id_type=MESH
        )

    def start(cond, *made):
        run(cond, lambda: copy(*made).start())
        sent.append((cond, made))

    def arrived(cond, target, send, recv, device):
        run(cond, lambda: copy(target, target, send, recv, device).wait_recv())

    def q_to_peers(cond, at, source):
        for step in range(1, groups):
            start(cond, source, q_part(at * 2 + core, group), qy_s.at[at, step], qy_r.at[at, step], peer(step))

    def q_to_partner(cond, at, part, source):
        start(cond, source, q_part(at * 2 + core, part), qc_s.at[at, part], qc_r.at[at, part], partner)

    def o_to_peers(cond, at, row, source):
        for step in range(1, groups):
            start(cond, source, o_part(at * 2 + core, row, group), oy_s.at[at, row, step], oy_r.at[at, row, step], peer(step))

    def o_to_partner(cond, at, row, part, source):
        start(cond, source, o_part(at * 2 + core, row, part), oc_s.at[at, row, part], oc_r.at[at, row, part], partner)

    def o_along_chip(cond, way, far, at, row, source):
        start(cond, source, o_part(at * 2 + core, row, group), ox_s.at[way, far, row], ox_r.at[way, far, row], along_chip(way))

    loads = [pltpu.make_async_copy(a, b, local.at[k]) for k, (a, b) in enumerate(((norm, n_all.at[place]), (wq, v_wq), (wo, v_wo)))]
    for load in loads:
        load.start()

    own_q = wq.at[pl.ds(pl.multiple_of(group * q_rows, 8), q_rows)]
    own_o = wo.at[pl.ds(pl.multiple_of(group * o_rows, 8), o_rows)]
    for way in (0, 1):
        go = goes_on(place, seqs, way)
        start(go, norm, n_all.at[place], nz_s.at[way, 1], nz_r.at[way, 1], along_seq(way))
        start(go, own_o, o_part(tile, place, group), oz_s.at[way, 1], oz_r.at[way, 1], along_seq(way))
        go = goes_on(chip, chips, way)
        start(go, own_q, q_part(tile, group), qx_s.at[way, 1], qx_r.at[way, 1], along_chip(way))
        o_along_chip(go, way, 1, chip, place, own_o)
    for part in range(groups):
        q_to_partner(None, chip, part, wq.at[pl.ds(part * q_rows, q_rows)])
        o_to_partner(None, chip, place, part, wo.at[pl.ds(part * o_rows, o_rows)])

    stores = [pltpu.make_async_copy(b, a, local.at[k]) for k, (a, b) in enumerate(((q_all.at[tile], v_wq), (o_all.at[tile, place], v_wo)))]
    for load in loads:
        load.wait()
    for store in stores:
        store.start()

    def rows_from_chips(rows):
        for far in range(1, chips):
            for way in (0, 1):
                at = chip - far if way == 0 else chip + far
                for given, row in rows:
                    here = arrives(chip, chips, way, far)
                    here = here if given is None else both(here, given)
                    piece = o_part(at * 2 + core, row, group)
                    arrived(here, piece, ox_s.at[way, far, row], ox_r.at[way, far, row], along_chip(way))
                    if far < chips - 1:
                        o_along_chip(both(here, goes_on(chip, chips, way)), way, far + 1, at, row, piece)
                    o_to_peers(here, at, row, piece)
                    o_to_partner(here, at, row, group, piece)

    def rows_at(far):
        if far == 0:
            return [(None, place)]
        return [(arrives(place, seqs, way, far), place - far if way == 0 else place + far) for way in (0, 1)]

    def out_step(far):
        for way in (0, 1):
            here = arrives(place, seqs, way, far)
            row = place - far if way == 0 else place + far
            piece = o_part(tile, row, group)
            arrived(here, piece, oz_s.at[way, far], oz_r.at[way, far], along_seq(way))
            if far < seqs - 1:
                start(both(here, goes_on(place, seqs, way)), piece, piece, oz_s.at[way, far + 1], oz_r.at[way, far + 1], along_seq(way))
            for side in (0, 1):
                o_along_chip(both(here, goes_on(chip, chips, side)), side, 1, chip, row, piece)
            o_to_peers(here, chip, row, piece)
            o_to_partner(here, chip, row, group, piece)

    def norm_step(far):
        for way in (0, 1):
            here = arrives(place, seqs, way, far)
            row = place - far if way == 0 else place + far
            piece = n_all.at[row]
            arrived(here, piece, nz_s.at[way, far], nz_r.at[way, far], along_seq(way))
            if far < seqs - 1:
                start(both(here, goes_on(place, seqs, way)), piece, piece, nz_s.at[way, far + 1], nz_r.at[way, far + 1], along_seq(way))

    def chip_step(far):
        for way in (0, 1):
            here = arrives(chip, chips, way, far)
            at = chip - far if way == 0 else chip + far
            piece = q_part(at * 2 + core, group)
            arrived(here, piece, qx_s.at[way, far], qx_r.at[way, far], along_chip(way))
            if far < chips - 1:
                start(both(here, goes_on(chip, chips, way)), piece, piece, qx_s.at[way, far + 1], qx_r.at[way, far + 1], along_chip(way))
            q_to_peers(here, at, piece)
            q_to_partner(here, at, group, piece)

    def q_from_peers():
        for step in range(1, groups):
            part = (group + groups - step) % groups
            for at in range(chips):
                away = chip != at
                piece = q_part(at * 2 + core, part)
                arrived(away, piece, qy_s.at[at, step], qy_r.at[at, step], partner)
                q_to_partner(away, at, part, piece)

    def o_from_peers():
        for step in range(1, groups):
            part = (group + groups - step) % groups
            for at in range(chips):
                for row in range(seqs):
                    away = jnp.logical_or(chip != at, place != row)
                    piece = o_part(at * 2 + core, row, part)
                    arrived(away, piece, oy_s.at[at, row, step], oy_r.at[at, row, step], partner)
                    o_to_partner(away, at, row, part, piece)

    last = max(chips, seqs) - 1
    for far in range(1, last + 1):
        if 1 < far < seqs:
            rows_from_chips(rows_at(far - 1))
        if far < seqs:
            norm_step(far)
        if far < seqs - 1:
            out_step(far)
        if far < chips:
            chip_step(far)
        if far == 1 and seqs > 1:
            rows_from_chips(rows_at(0))
        if far == max(chips - 1, min(2, last)):
            q_from_peers()
    for at in range(chips):
        for part in range(groups):
            arrived(None, q_part(at * 2 + other, part), qc_s.at[at, part], qc_r.at[at, part], partner)
    for store in stores:
        store.wait()

    heads = wq.shape[1] // (3 * HD)
    depth, block = wq.shape[0], norm.shape[0]

    def fetch(head):
        slot = head % 2
        columns = pl.ds(pl.multiple_of(head * (3 * HD), 128), 3 * HD)
        return [
            pltpu.make_async_copy(
                q_all.at[at, :, columns], w_head.at[slot, pl.ds(at * depth, depth)], w_sem.at[slot, at]
            )
            for at in range(2 * chips)
        ]

    def one_head(head, carry):
        for load in fetch(head):
            load.wait()

        @pl.when(head + 1 < heads)
        def _():
            for load in fetch(head + 1):
                load.start()

        weights = w_head.at[head % 2]
        for row in range(seqs):
            at = pl.ds(row * block, block)
            part = jnp.dot(n_all[row], weights[...], preferred_element_type=jnp.float32)
            queries[at, :] = root_norm(part[:, :HD]).astype(jnp.bfloat16)
            keys[at, :] = root_norm(part[:, HD : 2 * HD]).astype(jnp.bfloat16)
            values[at, :] = part[:, 2 * HD :].astype(jnp.bfloat16)
        for row in range(seqs):
            at = pl.ds(row * block, block)
            scores = lax.dot_general(
                queries[at, :], keys[...], (((1,), (1,)), ((), ())), preferred_element_type=jnp.float32
            )
            expo = jnp.exp(scores * scale)
            probs = (expo * (1.0 / jnp.sum(expo, axis=-1, keepdims=True))).astype(jnp.bfloat16)
            attended[at, pl.ds(pl.multiple_of(head * HD, 128), HD)] = jnp.dot(
                probs, values[...], preferred_element_type=jnp.float32
            ).astype(jnp.bfloat16)
        return carry

    def between(step):
        if step == 0 and seqs > 1:
            out_step(seqs - 1)
        if step == 1:
            rows_from_chips(rows_at(seqs - 1))
        if step == 2:
            o_from_peers()

    for load in fetch(0):
        load.start()
    cuts = [0, heads // 3, heads // 2, 5 * heads // 6, heads]
    for step in range(4):
        if cuts[step] < cuts[step + 1]:
            lax.fori_loop(cuts[step], cuts[step + 1], one_head, 0)
        between(step)

    for at in range(chips):
        for part in range(groups):
            for row in range(seqs):
                arrived(None, o_part(at * 2 + other, row, part), oc_s.at[at, row, part], oc_r.at[at, row, part], partner)
    for cond, made in sent:
        run(cond, lambda made=made: copy(*made).wait_send())


def gather(norm, wq, wo):
    groups, tiles, seqs = (lax.axis_size(name) for name in ("group", "tile", "seq"))
    chips = tiles // 2
    length = seqs * norm.shape[0]
    pairs = [(2, seqs), (2, seqs), (2, chips), (2, chips, seqs), (chips, groups), (chips, seqs, groups), (chips, groups), (chips, seqs, groups)]
    return pl.pallas_call(
        functools.partial(gather_kernel, groups, chips, seqs, 1.0 / math.sqrt(HD)),
        out_shape=(
            jax.ShapeDtypeStruct((tiles,) + wq.shape, wq.dtype),
            jax.ShapeDtypeStruct((tiles, seqs) + wo.shape, wo.dtype),
            jax.ShapeDtypeStruct((length, wq.shape[1] // 3), norm.dtype),
        ),
        in_specs=[pl.BlockSpec(memory_space=pl.ANY)] * 3,
        out_specs=(pl.BlockSpec(memory_space=pl.ANY),) * 2 + (pl.BlockSpec(memory_space=pltpu.VMEM),),
        scratch_shapes=[pltpu.VMEM((seqs,) + norm.shape, norm.dtype)]
        + [pltpu.VMEM(a.shape, a.dtype) for a in (wq, wo)]
        + [pltpu.VMEM((2, tiles * wq.shape[0], 3 * HD), wq.dtype)]
        + [pltpu.VMEM((length, HD), norm.dtype)] * 3
        + [pltpu.SemaphoreType.DMA((3,)), pltpu.SemaphoreType.DMA((2, tiles))]
        + [pltpu.SemaphoreType.DMA(shape) for shape in pairs for _ in range(2)],
        compiler_params=pltpu.CompilerParams(collective_id=0, has_side_effects=True),
    )(norm, wq, wo)


def tail_kernel(attended, blocks, hidden, modulation, w_head, velocity, summed):
    at = pl.program_id(0)
    width = blocks.shape[2]
    here = pl.ds(pl.multiple_of(at * width, 128), width)
    summed[:, here] = jnp.dot(attended[...], blocks[0], preferred_element_type=jnp.float32)

    @pl.when(at == pl.num_programs(0) - 1)
    def _():
        mixed = hidden[...].astype(jnp.float32) + modulation[2:3] * summed[...]
        norm_out = (layer_norm(mixed) * (1.0 + modulation[4:5]) + modulation[3:4]).astype(jnp.bfloat16)
        velocity[...] = jnp.dot(norm_out, w_head[...], preferred_element_type=jnp.float32)


def tail(attended, blocks, hidden, modulation, w_head):
    tiles, depth, width = blocks.shape
    if width % 128:
        summed = jnp.concatenate(
            [jnp.dot(attended, blocks[at], preferred_element_type=jnp.float32) for at in range(tiles)], axis=1
        )
        mixed = hidden.astype(jnp.float32) + modulation[2] * summed
        norm_out = (layer_norm(mixed) * (1.0 + modulation[4]) + modulation[3]).astype(jnp.bfloat16)
        return jnp.dot(norm_out, w_head, preferred_element_type=jnp.float32)
    whole = [pl.BlockSpec(a.shape, lambda at: (0, 0), pipeline_mode=pl.Buffered(1)) for a in (attended, hidden, modulation, w_head)]
    return pl.pallas_call(
        tail_kernel,
        grid=(tiles,),
        out_shape=jax.ShapeDtypeStruct((hidden.shape[0], w_head.shape[1]), jnp.float32),
        in_specs=[whole[0], pl.BlockSpec((1, depth, width), lambda at: (at, 0, 0)), *whole[1:]],
        out_specs=pl.BlockSpec((hidden.shape[0], w_head.shape[1]), lambda at: (0, 0)),
        scratch_shapes=[pltpu.VMEM(hidden.shape, jnp.float32)],
    )(attended, blocks, hidden, modulation, w_head)


def step_kernel(
    scale, hidden, wq, wo, mod_from, head_from, latent, weight, index, joined_out,
    n_all, normed, w_all, queries, keys, values, attended, att_in, o_all, summed,
    modulation, w_head, lat_in, wt_in, joint, msg, msg_in, result, local,
    nz_s, nz_r, qx_s, qx_r, qy_s, qy_r, qc_s, qc_r, qo_s, qo_r, oz_s, oz_r, ox_s, ox_r, oy_s, oy_r, oc_s, oc_r,
    at_s, at_r, ln_s, ln_r, wt_s, wt_r, ms_s, ms_r, rs_s, rs_r,
):
    group, tile, place = lax.axis_index("group"), lax.axis_index("tile"), lax.axis_index("seq")
    seqs, block, width = n_all.shape
    chip, core = tile // 2, tile % 2
    side = place // 2
    toward = 1 - 2 * side
    inner = jnp.logical_or(place == 1, place == 2)
    outer_end = jnp.logical_not(inner)
    over = (1 - chip) * 2 + core
    mate = chip * 2 + 1 - core
    mate_over = (1 - chip) * 2 + 1 - core
    x_dev, y_dev, p_dev, in_dev = {"tile": over}, {"group": 1 - group}, {"tile": mate}, {"seq": place + toward}
    out_dev = {"seq": place - toward}
    depth, cols = wq.shape
    q_half, o_half = depth // 2, wo.shape[0] // 2
    chunks = qx_s.shape[0]
    piece = q_half // chunks
    pairs = attended.shape[0]
    heads = queries.shape[0]
    both = jnp.logical_and

    def yes():
        return None

    def middle():
        return inner

    def ends():
        return outer_end

    def along(way):
        return {"seq": place + 1 - 2 * way}

    barrier = pltpu.get_barrier_semaphore()
    greet = [x_dev, y_dev, p_dev] + [{"seq": (place + far) % seqs} for far in range(1, seqs)]
    for device in greet:
        pl.semaphore_signal(barrier, inc=1, device_id=device, device_id_type=MESH)
    step_tile = 2 * side - 1
    tiles = lax.axis_size("tile")
    paired = jnp.logical_and(inner, jnp.logical_and(tile + step_tile >= 0, tile + step_tile < tiles))
    j_dev = {"tile": tile + step_tile, "seq": seqs - 1 - place}

    @pl.when(paired)
    def _():
        pl.semaphore_signal(barrier, inc=1, device_id=j_dev, device_id_type=MESH)

    pl.semaphore_wait(barrier, len(greet) + paired.astype(jnp.int32))

    sent = []

    def copy(source, target, send, recv, device):
        return pltpu.make_async_remote_copy(
            src_ref=source, dst_ref=target, send_sem=send, recv_sem=recv, device_id=device, device_id_type=MESH
        )

    def start(cond, make):
        run(cond(), lambda: copy(*make()).start())
        sent.append((cond, make))

    def arrived(cond, target, recv):
        run(cond, lambda: copy(target(), target(), recv, recv, p_dev).wait_recv())

    def w_rows(owner, part, at):
        return w_all.at[pl.ds(pl.multiple_of(owner * depth + part * q_half + at * piece, 16), piece)]

    def w_block(owner):
        return w_all.at[pl.ds(pl.multiple_of(owner * depth, 16), depth)]

    def o_rows(owner, kind, part):
        return o_all.at[owner, kind, pl.ds(pl.multiple_of(part * o_half, 16), o_half)]

    given = ((hidden, n_all.at[place]), (wq, w_block(tile)), (mod_from, modulation), (head_from, w_head))
    loads = [pltpu.make_async_copy(a, b, local.at[k]) for k, (a, b) in enumerate(given)]
    load_o = pltpu.make_async_copy(wo, o_all.at[tile, 0], local.at[len(loads)])
    for way in (0, 1):
        start(lambda way=way: goes_on(place, seqs, way), lambda way=way: (hidden, n_all.at[place], nz_s.at[way, 1], nz_r.at[way, 1], along(way)))
    for at in range(chunks):
        start(yes, lambda at=at: (
            wq.at[pl.ds(pl.multiple_of(group * q_half + at * piece, 16), piece)], w_rows(tile, group, at),
            qx_s.at[at], qx_r.at[at], x_dev))
    for load in loads:
        load.start()
    start(yes, lambda: (wq, w_block(tile), qo_s, qo_r, p_dev))
    start(middle, lambda: (wo, o_all.at[tile, 0], ox_s.at[0], ox_r.at[0], x_dev))
    start(ends, lambda: (wo, o_all.at[tile, 2], ox_s.at[2], ox_r.at[2], x_dev))
    start(ends, lambda: (wo, o_all.at[tile, 2], oz_s.at[0], oz_r.at[2], in_dev))
    start(ends, lambda: (latent, lat_in, ln_s, ln_r, in_dev))
    start(ends, lambda: (weight, wt_in, wt_s, wt_r, in_dev))
    run(inner, load_o.start)
    start(middle, lambda: (wo, o_all.at[tile, 0], oc_s.at[0, 0], oc_r.at[0, 0], p_dev))

    values[:, :, HD:] = jnp.ones((heads, values.shape[1], HD), values.dtype)

    def tokens(far):
        for way in (0, 1):
            here = arrives(place, seqs, way, far)
            row = functools.partial(lambda way: place - far if way == 0 else place + far, way)
            arrived(here, lambda row=row: n_all.at[row()], nz_r.at[way, far])
            if far < seqs - 1:
                start(
                    lambda way=way: both(arrives(place, seqs, way, far), goes_on(place, seqs, way)),
                    lambda row=row, way=way: (
                        n_all.at[row()], n_all.at[row()], nz_s.at[way, far + 1], nz_r.at[way, far + 1], along(way)))

    def q_over(at):
        arrived(None, lambda: w_rows(over, group, at), qx_r.at[at])
        start(yes, lambda: (w_rows(over, group, at), w_rows(over, group, at), qy_s.at[at], qy_r.at[at], y_dev))
        start(yes, lambda: (w_rows(over, group, at), w_rows(over, group, at), qc_s.at[0, at], qc_r.at[group, at], p_dev))

    def q_peer(at):
        arrived(None, lambda: w_rows(over, 1 - group, at), qy_r.at[at])
        start(yes, lambda: (
            w_rows(over, 1 - group, at), w_rows(over, 1 - group, at), qc_s.at[1, at], qc_r.at[1 - group, at], p_dev))

    def o_first():
        start(middle, lambda: (
            wo.at[pl.ds(pl.multiple_of(group * o_half, 16), o_half)], o_rows(tile, 1, group), oz_s.at[1], oz_r.at[1], in_dev))

    def o_end():
        arrived(outer_end, lambda: o_all.at[over, 2], ox_r.at[2])
        start(ends, lambda: (o_all.at[over, 2], o_all.at[over, 2], oz_s.at[3], oz_r.at[0], in_dev))
        arrived(inner, lambda: o_all.at[tile, 2], oz_r.at[2])
        start(middle, lambda: (o_rows(tile, 2, group), o_rows(tile, 3, group), oz_s.at[2], oz_r.at[3], in_dev))
        start(middle, lambda: (o_all.at[tile, 2], o_all.at[tile, 2], oc_s.at[0, 2], oc_r.at[0, 2], p_dev))

    def o_end_over():
        arrived(inner, lambda: o_all.at[over, 2], oz_r.at[0])
        start(middle, lambda: (o_all.at[over, 2], o_all.at[over, 2], oc_s.at[1, 2], oc_r.at[1, 2], p_dev))

    def o_chain(kind):
        arrived(inner, lambda: o_rows(tile, kind, group), oz_r.at[kind])
        start(middle, lambda: (o_rows(tile, kind, group), o_rows(tile, kind, group), ox_s.at[kind], ox_r.at[kind], x_dev))
        start(middle, lambda: (o_rows(tile, kind, group), o_rows(tile, kind, group), oy_s.at[0, kind], oy_r.at[0, kind], y_dev))

    def o_over(kind):
        if kind == 0:
            arrived(inner, lambda: o_all.at[over, 0], ox_r.at[0])
            start(middle, lambda: (o_all.at[over, 0], o_all.at[over, 0], oc_s.at[1, 0], oc_r.at[1, 0], p_dev))
        else:
            arrived(inner, lambda: o_rows(over, kind, group), ox_r.at[kind])
        if kind == 3:
            start(middle, lambda: (
                o_rows(over, kind, group), o_rows(over, kind, group), oy_s.at[1, kind], oy_r.at[1, kind], y_dev))

    def o_peer(kind):
        arrived(inner, lambda: o_rows(tile, kind, 1 - group), oy_r.at[0, kind])
        if kind == 1:
            start(middle, lambda: (
                o_rows(tile, kind, 1 - group), o_rows(tile, kind, 1 - group), oy_s.at[1, kind], oy_r.at[1, kind], x_dev))
        start(middle, lambda: (
            o_all.at[tile, kind], o_all.at[tile, kind], oc_s.at[0, kind], oc_r.at[0, kind], p_dev))

    def o_last(kind):
        arrived(inner, lambda: o_rows(over, kind, 1 - group), oy_r.at[1, kind])
        start(middle, lambda: (
            o_all.at[over, kind], o_all.at[over, kind], oc_s.at[1, kind], oc_r.at[1, kind], p_dev))

    q_over(0)
    for at in range(1, chunks):
        if at == chunks - 1:
            tokens(1)
            o_first()
        q_over(at)
        q_peer(at - 1)
    q_peer(chunks - 1)
    for load in loads:
        load.wait()
    arrived(None, lambda: w_block(mate), qo_r)
    for part in (0, 1):
        for at in range(chunks):
            arrived(None, lambda: w_rows(mate_over, part, at), qc_r.at[part, at])

    strip = 32

    def norm_of(row):
        def norm(at, carry):
            rows = pl.ds(pl.multiple_of(at * strip, strip), strip)
            given = n_all[row, rows, :].astype(jnp.float32)
            normed[rows, :] = (layer_norm(given) * (1.0 + modulation[1:2]) + modulation[0:1]).astype(normed.dtype)
            return carry

        lax.fori_loop(0, block // strip, norm, 0)

    def project(row, pair):
        place_of = pl.ds(pl.multiple_of(row * block, block), block)
        part = jnp.dot(
            normed[...], w_all[:, pl.ds(pl.multiple_of(pair * (6 * HD), 128), 6 * HD)], preferred_element_type=jnp.float32
        )
        for at in (0, 1):
            here = 3 * HD * at
            queries[2 * pair + at, place_of, :] = root_norm(part[:, here : here + HD]).astype(queries.dtype)
            keys[2 * pair + at, place_of, :] = root_norm(part[:, here + HD : here + 2 * HD]).astype(keys.dtype)
            values[2 * pair + at, place_of, pl.ds(0, HD)] = part[:, here + 2 * HD : here + 3 * HD].astype(values.dtype)

    final = (seqs - 1) * (1 - side)

    def in_order(step, carry):
        @pl.when(step == 1)
        def _():
            o_end()

        @pl.when(step == 2)
        def _():
            tokens(2)

        far, way = (step + 1) // 2, (step + 1) % 2
        row = place + far * (2 * way - 1)

        @pl.when(both(both(row >= 0, row < seqs), row != final))
        def _():
            norm_of(row)
            lax.fori_loop(0, pairs, lambda pair, carry: (project(row, pair), carry)[1], 0)

        return carry

    lax.fori_loop(0, 2 * seqs - 3, in_order, 0)
    o_over(0)
    tokens(3)
    norm_of(final)

    def leave(pair, turn):
        row = (turn + 2 * (1 - side)) % seqs
        target, slot = row // 2 + 1, 1 - ((row + 1) // 2) % 2
        kind = 2 * outer_end.astype(jnp.int32) + (side != row // 2).astype(jnp.int32)
        source = attended.at[pair, pl.ds(pl.multiple_of(row * block, block), block)]
        landing = att_in.at[kind, pair, pl.ds(pl.multiple_of(slot * block, block), block)]
        got = at_r.at[kind, slot, pair]

        def away():
            return copy(source, landing, at_s.at[turn, pair], got, {"seq": target})

        def stay():
            return pltpu.make_async_copy(source, landing, got)

        return row, place != target, away, stay

    def one_pair(pair, carry):
        project(final, pair)
        for turn in range(seqs):
            row, far, away, stay = leave(pair, turn)
            at = pl.ds(pl.multiple_of(row * block, block), block)
            for half in (0, 1):
                head = 2 * pair + half
                scores = lax.dot_general(
                    queries[head, at, :], keys[head], (((1,), (1,)), ((), ())), preferred_element_type=jnp.float32
                )
                expo = jnp.exp2(scores * scale).astype(jnp.bfloat16)
                mixed = jnp.dot(expo, values[head], preferred_element_type=jnp.float32)
                attended[pair, at, pl.ds(half * HD, HD)] = (mixed[:, :HD] * (1.0 / mixed[:, HD:])).astype(attended.dtype)
            run(far, lambda away=away: away().start())
            run(jnp.logical_not(far), lambda stay=stay: stay().start())

        @pl.when(pair == 0)
        def _():
            o_chain(1)

        @pl.when(pair == pairs - 1)
        def _():
            o_end_over()
            o_chain(3)

        return carry

    lax.fori_loop(0, pairs, one_pair, 0)

    run(inner, load_o.wait)

    def rows_here(kind):
        copy(o_all.at[mate, kind], o_all.at[mate, kind], oc_s.at[0, kind], oc_r.at[0, kind], p_dev).wait_recv()
        copy(o_all.at[mate_over, kind], o_all.at[mate_over, kind], oc_s.at[1, kind], oc_r.at[1, kind], p_dev).wait_recv()

    def attended_here(kind, slot, pair):
        landing = att_in.at[kind, pair, pl.ds(slot * block, block)]
        copy(landing, landing, at_r.at[kind, slot, pair], at_r.at[kind, slot, pair], p_dev).wait_recv()

    def add_up(kind, which, fresh=False):
        def columns(owner, carry):
            here = pl.ds(pl.multiple_of(owner * wo.shape[1], 128), wo.shape[1])
            total = 0.0 if fresh else summed[:, here]
            for pair in which:
                rows = pl.ds(pl.multiple_of(pair * 2 * HD, 2 * HD), 2 * HD)
                total += jnp.dot(att_in[kind, pair], o_all[owner, kind, rows, :], preferred_element_type=jnp.float32)
            summed[:, here] = total
            return carry

        lax.fori_loop(0, o_all.shape[0], columns, 0)

    @pl.when(inner)
    def _():
        rows_here(0)
        for slot in (0, 1):
            for pair in range(pairs):
                landing = att_in.at[0, pair, pl.ds(slot * block, block)]
                pltpu.make_async_copy(attended.at[pair, pl.ds(0, block)], landing, at_r.at[0, slot, pair]).wait()
        add_up(0, range(pairs), True)

    o_over(1)
    o_peer(1)
    o_over(3)
    o_peer(3)

    def accumulate(at, carry):
        pair, kind = at // 2, 2 + at % 2

        @pl.when(at == 1)
        def _():
            o_last(1)
            o_last(3)

            @pl.when(inner)
            def _():
                rows_here(1)
                for pair in range(pairs):
                    for slot in (0, 1):
                        attended_here(1, slot, pair)
                add_up(1, range(pairs))

        @pl.when(inner)
        def _():
            @pl.when(pair == 0)
            def _():
                rows_here(kind)

            for slot in (0, 1):
                attended_here(kind, slot, pair)
            add_up(kind, [pair])

        return carry

    lax.fori_loop(0, 2 * pairs, accumulate, 0)

    def message(slot):
        return copy(msg.at[slot], msg_in.at[1 - slot], ms_s.at[slot], ms_r.at[1 - slot], j_dev)

    def answer():
        return copy(result, result, rs_s, rs_r, out_dev)

    channels = latent.shape[0]

    def level(offset):
        at = jnp.broadcast_to(index[...].astype(jnp.float32), (1, block)) + offset
        return noise_level(at, NSTEPS)

    @pl.when(inner)
    def _():
        copy(latent, lat_in, ln_s, ln_r, p_dev).wait_recv()
        copy(weight, wt_in, wt_s, wt_r, p_dev).wait_recv()
        now, after = level(0.0), level(1.0)
        for slot in (0, 1):
            row = place - toward * slot

            def norm(at, carry):
                rows = pl.ds(pl.multiple_of(at * strip, strip), strip)
                sums = pl.ds(pl.multiple_of(slot * block + at * strip, strip), strip)
                mixed = n_all[row, rows, :].astype(jnp.float32) + modulation[2:3] * summed[sums, :]
                normed[rows, :] = (layer_norm(mixed) * (1.0 + modulation[4:5]) + modulation[3:4]).astype(normed.dtype)
                return carry

            lax.fori_loop(0, block // strip, norm, 0)
            velocity = lax.dot_general(
                w_head[...], normed[...], (((1,), (1,)), ((), ())), preferred_element_type=jnp.float32
            )
            base = (latent if slot == 0 else lat_in)[...]
            weighs = (weight if slot == 0 else wt_in)[...].astype(jnp.float32)
            joint[slot, pl.ds(0, channels), :] = (base + (after - now) * velocity) * weighs
            joint[slot, pl.ds(channels, channels), :] = (base - now * velocity) * weighs
            msg[slot, pl.ds(0, 2 * channels), :] = joint[slot].astype(msg.dtype)
            msg[slot, pl.ds(2 * channels, 16), :] = jnp.broadcast_to(weighs, (16, block)).astype(msg.dtype)
            run(paired, lambda slot=slot: message(slot).start())

        @pl.when(jnp.logical_not(paired))
        def _():
            msg_in[...] = jnp.zeros_like(msg_in)

        for slot in (1, 0):
            run(paired, lambda slot=slot: message(1 - slot).wait_recv())
            weighs = (weight if slot == 0 else wt_in)[...].astype(jnp.float32)
            given = msg_in[slot].astype(jnp.float32)
            joined = (joint[slot] + given[: 2 * channels]) / (weighs + given[2 * channels : 2 * channels + 1])
            if slot == 1:
                joint[1] = joined
                copy(joint.at[1], result, rs_s, rs_r, out_dev).start()
            else:
                joined_out[...] = joined
        for slot in (1, 0):
            run(paired, lambda slot=slot: message(slot).wait_send())
        copy(joint.at[1], result, rs_s, rs_r, out_dev).wait_send()

    @pl.when(outer_end)
    def _():
        answer().wait_recv()
        joined_out[...] = result[...]

    def drain(pair, carry):
        for turn in range(seqs):
            _, far, away, _ = leave(pair, turn)
            run(far, lambda away=away: away().wait_send())
        return carry

    lax.fori_loop(0, pairs, drain, 0)
    for cond, make in sent:
        run(cond(), lambda make=make: copy(*make()).wait_send())


def fused(hidden, wq, wo, modulation, w_head, latent, weight, index):
    tiles, seqs = lax.axis_size("tile"), lax.axis_size("seq")
    block, width = hidden.shape
    length, heads = seqs * block, wq.shape[1] // (3 * HD)
    pairs, chunks = heads // 2, 3
    channels = w_head.shape[0]
    sizes = [(2, seqs)] * 2 + [(chunks,)] * 4 + [(2, chunks)] * 2 + [()] * 2 + [(4,)] * 4 + [(2, 4)] * 4
    sizes += [(seqs, pairs), (4, 2, pairs)] + [()] * 4 + [(2,)] * 2 + [()] * 2
    any_space, vmem = pl.BlockSpec(memory_space=pl.ANY), pl.BlockSpec(memory_space=pltpu.VMEM)
    return pl.pallas_call(
        functools.partial(step_kernel, math.log2(math.e) / math.sqrt(HD)),
        out_shape=jax.ShapeDtypeStruct((2 * channels, block), jnp.float32),
        in_specs=[any_space] * 5 + [vmem] * 3,
        out_specs=vmem,
        scratch_shapes=[
            pltpu.VMEM((seqs, block, width), hidden.dtype),
            pltpu.VMEM((block, width), hidden.dtype),
            pltpu.VMEM((tiles * wq.shape[0], wq.shape[1]), wq.dtype),
            pltpu.VMEM((heads, length, HD), hidden.dtype),
            pltpu.VMEM((heads, length, HD), hidden.dtype),
            pltpu.VMEM((heads, length, 2 * HD), hidden.dtype),
            pltpu.VMEM((pairs, length, 2 * HD), hidden.dtype),
            pltpu.VMEM((4, pairs, 2 * block, 2 * HD), hidden.dtype),
            pltpu.VMEM((tiles, 4) + wo.shape, wo.dtype),
            pltpu.VMEM((2 * block, width), jnp.float32),
            pltpu.VMEM(modulation.shape, modulation.dtype),
            pltpu.VMEM(w_head.shape, w_head.dtype),
            pltpu.VMEM((channels, block), jnp.float32),
            pltpu.VMEM((1, block), jnp.int32),
            pltpu.VMEM((2, 2 * channels, block), jnp.float32),
            pltpu.VMEM((2, 2 * channels + 16, block), jnp.bfloat16),
            pltpu.VMEM((2, 2 * channels + 16, block), jnp.bfloat16),
            pltpu.VMEM((2 * channels, block), jnp.float32),
            pltpu.SemaphoreType.DMA((5,)),
        ]
        + [pltpu.SemaphoreType.DMA(shape) for shape in sizes],
        compiler_params=pltpu.CompilerParams(collective_id=1, has_side_effects=True, vmem_limit_bytes=67043328),
    )(hidden, wq, wo, modulation, w_head, latent, weight, index)


def fits(hidden, w_qkv, w_out):
    sizes = tuple(lax.axis_size(name) for name in ("group", "tile", "seq"))
    heads = w_qkv.shape[1] // (3 * HD)
    return sizes == (2, 4, 4) and heads % 2 == 0 and w_out.shape[1] % 128 == 0 and w_qkv.shape[0] % 96 == 0


def spread(hidden, modulation, w_qkv, w_out, w_head):
    local = hidden[0].astype(jnp.float32)
    norm_in = (layer_norm(local) * (1.0 + modulation[1]) + modulation[0]).astype(jnp.bfloat16)
    _, out_blocks, attended = gather(norm_in, w_qkv, w_out)
    attended = lax.all_to_all(attended, "seq", split_axis=0, concat_axis=1, tiled=True)
    out_blocks = out_blocks.reshape(out_blocks.shape[0], -1, out_blocks.shape[3])
    return tail(attended, out_blocks, hidden[0], modulation, w_head)


def shards(hidden, modulation, w_qkv, w_out, w_head, latent, weights_int, step_index):
    if fits(hidden, w_qkv, w_out):
        joined = fused(hidden[0], w_qkv, w_out, modulation, w_head.T, latent[0].T, weights_int, step_index[None])
        channels = latent.shape[2]
        return (joined[:channels].T[None], joined[channels:].T[None])
    velocity = spread(hidden, modulation, w_qkv, w_out, w_head).T
    index = step_index[0].astype(jnp.float32)
    now = noise_level(index, NSTEPS)
    after = noise_level(index + 1.0, NSTEPS)
    base = latent[0].T
    weight = weights_int[0].astype(jnp.float32)
    moved = base + (after - now) * velocity
    guess = base - now * velocity
    weighted = jnp.concatenate([moved, guess], axis=0) * weight[None, :]
    seq_count, tile_count = lax.axis_size("seq"), lax.axis_size("tile")
    jump = seq_count - 2
    moves = [
        (t * seq_count + s, (t + 1) * seq_count + s - jump)
        for t in range(tile_count - 1)
        for s in range(jump, seq_count)
    ]
    moves = moves + [(there, here) for here, there in moves]
    other_sums = lax.ppermute(weighted.astype(jnp.bfloat16), ("tile", "seq"), moves)
    other_weight = lax.ppermute(weight.astype(jnp.bfloat16), ("tile", "seq"), moves)
    totals = weighted + other_sums.astype(jnp.float32)
    norms = weight + other_weight.astype(jnp.float32)
    joined = totals / norms[None, :]
    channels = velocity.shape[0]
    return (joined[:channels].T[None], joined[channels:].T[None])


def solution(mesh):
    in_specs = (
        P(("group", "tile"), "seq", None),
        P("group", None),
        P("tile", "seq"),
        P("seq", "tile"),
        P(),
        P(("group", "tile"), "seq", None),
        P(("group", "tile"), "seq"),
        P("group"),
    )
    out_specs = (P(("group", "tile"), "seq", None), P(("group", "tile"), "seq", None))
    return jax.shard_map(shards, mesh=mesh, in_specs=in_specs, out_specs=out_specs, check_vma=False)
```

```python
import functools
import math

import jax
import jax.numpy as jnp
from jax import lax
from jax.experimental import pallas as pl
from jax.experimental.pallas import tpu as pltpu
from jax.sharding import PartitionSpec as P

HD = 128
NSTEPS = 28


def layer_norm(values):
    mean = jnp.mean(values, axis=-1, keepdims=True)
    centred = values - mean
    spread = jnp.mean(centred * centred, axis=-1, keepdims=True)
    return centred * lax.rsqrt(spread + 1e-06)


def root_norm(values):
    return values * lax.rsqrt(jnp.mean(values * values, axis=-1, keepdims=True) + 1e-06)


def noise_level(index, steps):
    level = 1.0 - index / steps
    return 3.0 * level / (1.0 + 2.0 * level)


MESH = pl.DeviceIdType.MESH


def run(cond, body):
    if cond is None:
        body()
    else:
        pl.when(cond)(body)


def arrives(place, count, way, far):
    return place >= far if way == 0 else place <= count - 1 - far


def goes_on(place, count, way):
    return place < count - 1 if way == 0 else place > 0


def gather_kernel(
    groups, chips, seqs, scale, norm, wq, wo, q_all, o_all, attended,
    n_all, v_wq, v_wo, w_head, queries, keys, values, local, w_sem,
    nz_s, nz_r, oz_s, oz_r, qx_s, qx_r, ox_s, ox_r, qy_s, qy_r, oy_s, oy_r, qc_s, qc_r, oc_s, oc_r,
):
    group, tile, place = lax.axis_index("group"), lax.axis_index("tile"), lax.axis_index("seq")
    chip, core = tile // 2, tile % 2
    other = 1 - core
    partner = {"tile": chip * 2 + other}
    q_rows, o_rows = wq.shape[0] // groups, wo.shape[0] // groups
    both = jnp.logical_and

    def q_part(owner, part):
        return q_all.at[owner, pl.ds(pl.multiple_of(part * q_rows, 8), q_rows)]

    def o_part(owner, row, part):
        return o_all.at[owner, row, pl.ds(pl.multiple_of(part * o_rows, 8), o_rows)]

    def along_seq(way):
        return {"seq": place + 1 - 2 * way}

    def along_chip(way):
        return {"tile": tile + 2 - 4 * way}

    def peer(step):
        return {"group": (group + step) % groups}

    barrier = pltpu.get_barrier_semaphore()
    greet = [(goes_on(place, seqs, way), along_seq(way)) for way in (0, 1)]
    greet += [(goes_on(chip, chips, way), along_chip(way)) for way in (0, 1)]
    greet += [(None, peer(step)) for step in range(1, groups)] + [(None, partner)]
    for cond, device in greet:
        run(cond, lambda device=device: pl.semaphore_signal(barrier, inc=1, device_id=device, device_id_type=MESH))
    met = groups + sum(goes_on(at, count, way).astype(jnp.int32) for at, count in ((place, seqs), (chip, chips)) for way in (0, 1))
    pl.semaphore_wait(barrier, met)

    sent = []

    def copy(source, target, send, recv, device):
        return pltpu.make_async_remote_copy(
            src_ref=source, dst_ref=target, send_sem=send, recv_sem=recv, device_id=device, device_id_type=MESH
        )

    def start(cond, *made):
        run(cond, lambda: copy(*made).start())
        sent.append((cond, made))

    def arrived(cond, target, send, recv, device):
        run(cond, lambda: copy(target, target, send, recv, device).wait_recv())

    def q_to_peers(cond, at, source):
        for step in range(1, groups):
            start(cond, source, q_part(at * 2 + core, group), qy_s.at[at, step], qy_r.at[at, step], peer(step))

    def q_to_partner(cond, at, part, source):
        start(cond, source, q_part(at * 2 + core, part), qc_s.at[at, part], qc_r.at[at, part], partner)

    def o_to_peers(cond, at, row, source):
        for step in range(1, groups):
            start(cond, source, o_part(at * 2 + core, row, group), oy_s.at[at, row, step], oy_r.at[at, row, step], peer(step))

    def o_to_partner(cond, at, row, part, source):
        start(cond, source, o_part(at * 2 + core, row, part), oc_s.at[at, row, part], oc_r.at[at, row, part], partner)

    def o_along_chip(cond, way, far, at, row, source):
        start(cond, source, o_part(at * 2 + core, row, group), ox_s.at[way, far, row], ox_r.at[way, far, row], along_chip(way))

    loads = [pltpu.make_async_copy(a, b, local.at[k]) for k, (a, b) in enumerate(((norm, n_all.at[place]), (wq, v_wq), (wo, v_wo)))]
    for load in loads:
        load.start()

    own_q = wq.at[pl.ds(pl.multiple_of(group * q_rows, 8), q_rows)]
    own_o = wo.at[pl.ds(pl.multiple_of(group * o_rows, 8), o_rows)]
    for way in (0, 1):
        go = goes_on(place, seqs, way)
        start(go, norm, n_all.at[place], nz_s.at[way, 1], nz_r.at[way, 1], along_seq(way))
        start(go, own_o, o_part(tile, place, group), oz_s.at[way, 1], oz_r.at[way, 1], along_seq(way))
        go = goes_on(chip, chips, way)
        start(go, own_q, q_part(tile, group), qx_s.at[way, 1], qx_r.at[way, 1], along_chip(way))
        o_along_chip(go, way, 1, chip, place, own_o)
    for part in range(groups):
        q_to_partner(None, chip, part, wq.at[pl.ds(part * q_rows, q_rows)])
        o_to_partner(None, chip, place, part, wo.at[pl.ds(part * o_rows, o_rows)])

    stores = [pltpu.make_async_copy(b, a, local.at[k]) for k, (a, b) in enumerate(((q_all.at[tile], v_wq), (o_all.at[tile, place], v_wo)))]
    for load in loads:
        load.wait()
    for store in stores:
        store.start()

    def rows_from_chips(rows):
        for far in range(1, chips):
            for way in (0, 1):
                at = chip - far if way == 0 else chip + far
                for given, row in rows:
                    here = arrives(chip, chips, way, far)
                    here = here if given is None else both(here, given)
                    piece = o_part(at * 2 + core, row, group)
                    arrived(here, piece, ox_s.at[way, far, row], ox_r.at[way, far, row], along_chip(way))
                    if far < chips - 1:
                        o_along_chip(both(here, goes_on(chip, chips, way)), way, far + 1, at, row, piece)
                    o_to_peers(here, at, row, piece)
                    o_to_partner(here, at, row, group, piece)

    def rows_at(far):
        if far == 0:
            return [(None, place)]
        return [(arrives(place, seqs, way, far), place - far if way == 0 else place + far) for way in (0, 1)]

    def out_step(far):
        for way in (0, 1):
            here = arrives(place, seqs, way, far)
            row = place - far if way == 0 else place + far
            piece = o_part(tile, row, group)
            arrived(here, piece, oz_s.at[way, far], oz_r.at[way, far], along_seq(way))
            if far < seqs - 1:
                start(both(here, goes_on(place, seqs, way)), piece, piece, oz_s.at[way, far + 1], oz_r.at[way, far + 1], along_seq(way))
            for side in (0, 1):
                o_along_chip(both(here, goes_on(chip, chips, side)), side, 1, chip, row, piece)
            o_to_peers(here, chip, row, piece)
            o_to_partner(here, chip, row, group, piece)

    def norm_step(far):
        for way in (0, 1):
            here = arrives(place, seqs, way, far)
            row = place - far if way == 0 else place + far
            piece = n_all.at[row]
            arrived(here, piece, nz_s.at[way, far], nz_r.at[way, far], along_seq(way))
            if far < seqs - 1:
                start(both(here, goes_on(place, seqs, way)), piece, piece, nz_s.at[way, far + 1], nz_r.at[way, far + 1], along_seq(way))

    def chip_step(far):
        for way in (0, 1):
            here = arrives(chip, chips, way, far)
            at = chip - far if way == 0 else chip + far
            piece = q_part(at * 2 + core, group)
            arrived(here, piece, qx_s.at[way, far], qx_r.at[way, far], along_chip(way))
            if far < chips - 1:
                start(both(here, goes_on(chip, chips, way)), piece, piece, qx_s.at[way, far + 1], qx_r.at[way, far + 1], along_chip(way))
            q_to_peers(here, at, piece)
            q_to_partner(here, at, group, piece)

    def q_from_peers():
        for step in range(1, groups):
            part = (group + groups - step) % groups
            for at in range(chips):
                away = chip != at
                piece = q_part(at * 2 + core, part)
                arrived(away, piece, qy_s.at[at, step], qy_r.at[at, step], partner)
                q_to_partner(away, at, part, piece)

    def o_from_peers():
        for step in range(1, groups):
            part = (group + groups - step) % groups
            for at in range(chips):
                for row in range(seqs):
                    away = jnp.logical_or(chip != at, place != row)
                    piece = o_part(at * 2 + core, row, part)
                    arrived(away, piece, oy_s.at[at, row, step], oy_r.at[at, row, step], partner)
                    o_to_partner(away, at, row, part, piece)

    last = max(chips, seqs) - 1
    for far in range(1, last + 1):
        if 1 < far < seqs:
            rows_from_chips(rows_at(far - 1))
        if far < seqs:
            norm_step(far)
        if far < seqs - 1:
            out_step(far)
        if far < chips:
            chip_step(far)
        if far == 1 and seqs > 1:
            rows_from_chips(rows_at(0))
        if far == max(chips - 1, min(2, last)):
            q_from_peers()
    for at in range(chips):
        for part in range(groups):
            arrived(None, q_part(at * 2 + other, part), qc_s.at[at, part], qc_r.at[at, part], partner)
    for store in stores:
        store.wait()

    heads = wq.shape[1] // (3 * HD)
    depth, block = wq.shape[0], norm.shape[0]

    def fetch(head):
        slot = head % 2
        columns = pl.ds(pl.multiple_of(head * (3 * HD), 128), 3 * HD)
        return [
            pltpu.make_async_copy(
                q_all.at[at, :, columns], w_head.at[slot, pl.ds(at * depth, depth)], w_sem.at[slot, at]
            )
            for at in range(2 * chips)
        ]

    def one_head(head, carry):
        for load in fetch(head):
            load.wait()

        @pl.when(head + 1 < heads)
        def _():
            for load in fetch(head + 1):
                load.start()

        weights = w_head.at[head % 2]
        for row in range(seqs):
            at = pl.ds(row * block, block)
            part = jnp.dot(n_all[row], weights[...], preferred_element_type=jnp.float32)
            queries[at, :] = root_norm(part[:, :HD]).astype(jnp.bfloat16)
            keys[at, :] = root_norm(part[:, HD : 2 * HD]).astype(jnp.bfloat16)
            values[at, :] = part[:, 2 * HD :].astype(jnp.bfloat16)
        for row in range(seqs):
            at = pl.ds(row * block, block)
            scores = lax.dot_general(
                queries[at, :], keys[...], (((1,), (1,)), ((), ())), preferred_element_type=jnp.float32
            )
            expo = jnp.exp(scores * scale)
            probs = (expo * (1.0 / jnp.sum(expo, axis=-1, keepdims=True))).astype(jnp.bfloat16)
            attended[at, pl.ds(pl.multiple_of(head * HD, 128), HD)] = jnp.dot(
                probs, values[...], preferred_element_type=jnp.float32
            ).astype(jnp.bfloat16)
        return carry

    def between(step):
        if step == 0 and seqs > 1:
            out_step(seqs - 1)
        if step == 1:
            rows_from_chips(rows_at(seqs - 1))
        if step == 2:
            o_from_peers()

    for load in fetch(0):
        load.start()
    cuts = [0, heads // 3, heads // 2, 5 * heads // 6, heads]
    for step in range(4):
        if cuts[step] < cuts[step + 1]:
            lax.fori_loop(cuts[step], cuts[step + 1], one_head, 0)
        between(step)

    for at in range(chips):
        for part in range(groups):
            for row in range(seqs):
                arrived(None, o_part(at * 2 + other, row, part), oc_s.at[at, row, part], oc_r.at[at, row, part], partner)
    for cond, made in sent:
        run(cond, lambda made=made: copy(*made).wait_send())


def gather(norm, wq, wo):
    groups, tiles, seqs = (lax.axis_size(name) for name in ("group", "tile", "seq"))
    chips = tiles // 2
    length = seqs * norm.shape[0]
    pairs = [(2, seqs), (2, seqs), (2, chips), (2, chips, seqs), (chips, groups), (chips, seqs, groups), (chips, groups), (chips, seqs, groups)]
    return pl.pallas_call(
        functools.partial(gather_kernel, groups, chips, seqs, 1.0 / math.sqrt(HD)),
        out_shape=(
            jax.ShapeDtypeStruct((tiles,) + wq.shape, wq.dtype),
            jax.ShapeDtypeStruct((tiles, seqs) + wo.shape, wo.dtype),
            jax.ShapeDtypeStruct((length, wq.shape[1] // 3), norm.dtype),
        ),
        in_specs=[pl.BlockSpec(memory_space=pl.ANY)] * 3,
        out_specs=(pl.BlockSpec(memory_space=pl.ANY),) * 2 + (pl.BlockSpec(memory_space=pltpu.VMEM),),
        scratch_shapes=[pltpu.VMEM((seqs,) + norm.shape, norm.dtype)]
        + [pltpu.VMEM(a.shape, a.dtype) for a in (wq, wo)]
        + [pltpu.VMEM((2, tiles * wq.shape[0], 3 * HD), wq.dtype)]
        + [pltpu.VMEM((length, HD), norm.dtype)] * 3
        + [pltpu.SemaphoreType.DMA((3,)), pltpu.SemaphoreType.DMA((2, tiles))]
        + [pltpu.SemaphoreType.DMA(shape) for shape in pairs for _ in range(2)],
        compiler_params=pltpu.CompilerParams(collective_id=0, has_side_effects=True),
    )(norm, wq, wo)


def tail_kernel(attended, blocks, hidden, modulation, w_head, velocity, summed):
    at = pl.program_id(0)
    width = blocks.shape[2]
    here = pl.ds(pl.multiple_of(at * width, 128), width)
    summed[:, here] = jnp.dot(attended[...], blocks[0], preferred_element_type=jnp.float32)

    @pl.when(at == pl.num_programs(0) - 1)
    def _():
        mixed = hidden[...].astype(jnp.float32) + modulation[2:3] * summed[...]
        norm_out = (layer_norm(mixed) * (1.0 + modulation[4:5]) + modulation[3:4]).astype(jnp.bfloat16)
        velocity[...] = jnp.dot(norm_out, w_head[...], preferred_element_type=jnp.float32)


def tail(attended, blocks, hidden, modulation, w_head):
    tiles, depth, width = blocks.shape
    if width % 128:
        summed = jnp.concatenate(
            [jnp.dot(attended, blocks[at], preferred_element_type=jnp.float32) for at in range(tiles)], axis=1
        )
        mixed = hidden.astype(jnp.float32) + modulation[2] * summed
        norm_out = (layer_norm(mixed) * (1.0 + modulation[4]) + modulation[3]).astype(jnp.bfloat16)
        return jnp.dot(norm_out, w_head, preferred_element_type=jnp.float32)
    whole = [pl.BlockSpec(a.shape, lambda at: (0, 0), pipeline_mode=pl.Buffered(1)) for a in (attended, hidden, modulation, w_head)]
    return pl.pallas_call(
        tail_kernel,
        grid=(tiles,),
        out_shape=jax.ShapeDtypeStruct((hidden.shape[0], w_head.shape[1]), jnp.float32),
        in_specs=[whole[0], pl.BlockSpec((1, depth, width), lambda at: (at, 0, 0)), *whole[1:]],
        out_specs=pl.BlockSpec((hidden.shape[0], w_head.shape[1]), lambda at: (0, 0)),
        scratch_shapes=[pltpu.VMEM(hidden.shape, jnp.float32)],
    )(attended, blocks, hidden, modulation, w_head)


def step_kernel(
    scale, hidden, wq, wo, mod_from, head_from, latent, weight, index, joined_out,
    n_all, normed, w_all, w_more, queries, keys, values, attended, att_in, o_all, summed,
    modulation, w_head, lat_in, wt_in, joint, msg, msg_in, result, local,
    nz_s, nz_r, qx_s, qx_r, qy_s, qy_r, qc_s, qc_r, qo_s, qo_r, oz_s, oz_r, ox_s, ox_r, oy_s, oy_r, oc_s, oc_r, ex_s, ex_r,
    at_s, at_r, ln_s, ln_r, wt_s, wt_r, ms_s, ms_r, rs_s, rs_r,
):
    group, tile, place = lax.axis_index("group"), lax.axis_index("tile"), lax.axis_index("seq")
    seqs, block, width = n_all.shape
    chip, core = tile // 2, tile % 2
    side = place // 2
    toward = 1 - 2 * side
    inner = jnp.logical_or(place == 1, place == 2)
    outer_end = jnp.logical_not(inner)
    over = (1 - chip) * 2 + core
    mate = chip * 2 + 1 - core
    mate_over = (1 - chip) * 2 + 1 - core
    x_dev, y_dev, p_dev, in_dev = {"tile": over}, {"group": 1 - group}, {"tile": mate}, {"seq": place + toward}
    out_dev = {"seq": place - toward}
    depth, cols = wq.shape
    q_half, o_half = depth // 2, wo.shape[0] // 2
    chunks = qx_s.shape[0]
    piece = q_half // chunks
    pairs = attended.shape[0] - 1
    heads = queries.shape[0]
    both = jnp.logical_and

    def yes():
        return None

    def middle():
        return inner

    def ends():
        return outer_end

    def along(way):
        return {"seq": place + 1 - 2 * way}

    barrier = pltpu.get_barrier_semaphore()
    greet = [x_dev, y_dev, p_dev] + [{"seq": (place + far) % seqs} for far in range(1, seqs)]
    for device in greet:
        pl.semaphore_signal(barrier, inc=1, device_id=device, device_id_type=MESH)
    step_tile = 2 * side - 1
    tiles = lax.axis_size("tile")
    paired = jnp.logical_and(inner, jnp.logical_and(tile + step_tile >= 0, tile + step_tile < tiles))
    j_dev = {"tile": tile + step_tile, "seq": seqs - 1 - place}

    @pl.when(paired)
    def _():
        pl.semaphore_signal(barrier, inc=1, device_id=j_dev, device_id_type=MESH)

    pl.semaphore_wait(barrier, len(greet) + paired.astype(jnp.int32))

    sent = []

    def copy(source, target, send, recv, device):
        return pltpu.make_async_remote_copy(
            src_ref=source, dst_ref=target, send_sem=send, recv_sem=recv, device_id=device, device_id_type=MESH
        )

    def start(cond, make):
        run(cond(), lambda: copy(*make()).start())
        sent.append((cond, make))

    def arrived(cond, target, recv):
        run(cond, lambda: copy(target(), target(), recv, recv, p_dev).wait_recv())

    def w_rows(owner, part, at):
        return w_all.at[pl.ds(pl.multiple_of(owner * depth + part * q_half + at * piece, 16), piece)]

    def w_block(owner):
        return w_all.at[pl.ds(pl.multiple_of(owner * depth, 16), depth)]

    def more_block(owner):
        return w_more.at[pl.ds(pl.multiple_of(owner * depth, 16), depth)]

    def o_rows(owner, kind, part):
        return o_all.at[owner, kind, pl.ds(pl.multiple_of(part * o_half, 16), o_half)]

    def wo_half(part):
        return wo.at[pl.ds(pl.multiple_of(part * o_half, 16), o_half)]

    given = ((hidden, n_all.at[place]), (wq, w_block(tile)), (mod_from, modulation), (head_from, w_head))
    loads = [pltpu.make_async_copy(a, b, local.at[k]) for k, (a, b) in enumerate(given)]
    load_o = pltpu.make_async_copy(wo, o_all.at[tile, 0], local.at[len(loads)])
    for way in (0, 1):
        start(lambda way=way: goes_on(place, seqs, way), lambda way=way: (hidden, n_all.at[place], nz_s.at[way, 1], nz_r.at[way, 1], along(way)))
    for at in range(chunks):
        start(yes, lambda at=at: (
            wq.at[pl.ds(pl.multiple_of(group * q_half + at * piece, 16), piece)], w_rows(tile, group, at),
            qx_s.at[at], qx_r.at[at], x_dev))
    for load in loads:
        load.start()
    start(yes, lambda: (wq, w_block(tile), qo_s, qo_r, p_dev))
    start(middle, lambda: (wo_half(group), o_rows(tile, 0, group), ox_s.at[0], ox_r.at[0], x_dev))
    start(ends, lambda: (wo, o_all.at[tile, 2], ox_s.at[2], ox_r.at[2], x_dev))
    start(ends, lambda: (wq.at[:, pl.ds((pairs - 1) * 6 * HD, 6 * HD)], more_block(tile), ex_s.at[0], ex_r.at[0], in_dev))
    start(ends, lambda: (wo_half(group), o_rows(tile, 2, group), oz_s.at[0], oz_r.at[2], in_dev))
    start(ends, lambda: (wo_half(1 - group), o_rows(tile, 2, 1 - group), ex_s.at[4], ex_r.at[4], in_dev))
    start(ends, lambda: (latent, lat_in, ln_s, ln_r, in_dev))
    start(ends, lambda: (weight, wt_in, wt_s, wt_r, in_dev))
    run(inner, load_o.start)
    start(middle, lambda: (wo, o_all.at[tile, 0], oc_s.at[0, 0], oc_r.at[0, 0], p_dev))

    values[:, :, HD:] = jnp.ones((heads, values.shape[1], HD), values.dtype)

    def tokens(far):
        for way in (0, 1):
            here = arrives(place, seqs, way, far)
            row = functools.partial(lambda way: place - far if way == 0 else place + far, way)
            arrived(here, lambda row=row: n_all.at[row()], nz_r.at[way, far])
            if far < seqs - 1:
                start(
                    lambda way=way: both(arrives(place, seqs, way, far), goes_on(place, seqs, way)),
                    lambda row=row, way=way: (
                        n_all.at[row()], n_all.at[row()], nz_s.at[way, far + 1], nz_r.at[way, far + 1], along(way)))

    def q_over(at):
        arrived(None, lambda: w_rows(over, group, at), qx_r.at[at])
        start(yes, lambda: (w_rows(over, group, at), w_rows(over, group, at), qy_s.at[at], qy_r.at[at], y_dev))
        start(yes, lambda: (w_rows(over, group, at), w_rows(over, group, at), qc_s.at[0, at], qc_r.at[group, at], p_dev))

    def q_peer(at):
        arrived(None, lambda: w_rows(over, 1 - group, at), qy_r.at[at])
        start(yes, lambda: (
            w_rows(over, 1 - group, at), w_rows(over, 1 - group, at), qc_s.at[1, at], qc_r.at[1 - group, at], p_dev))

    def o_first():
        start(middle, lambda: (wo_half(group), o_rows(tile, 1, group), oz_s.at[1], oz_r.at[1], in_dev))

    def more():
        arrived(inner, lambda: more_block(tile), ex_r.at[0])
        start(middle, lambda: (more_block(tile), more_block(tile), ex_s.at[1], ex_r.at[1], x_dev))
        start(middle, lambda: (more_block(tile), more_block(tile), ex_s.at[2], ex_r.at[2], p_dev))

    def more_over():
        arrived(inner, lambda: more_block(over), ex_r.at[1])
        start(middle, lambda: (more_block(over), more_block(over), ex_s.at[3], ex_r.at[3], p_dev))

    def o_end():
        arrived(outer_end, lambda: o_all.at[over, 2], ox_r.at[2])
        start(ends, lambda: (o_all.at[over, 2], o_all.at[over, 2], oz_s.at[3], oz_r.at[0], in_dev))

    def o_end_far():
        arrived(inner, lambda: o_rows(tile, 2, group), oz_r.at[2])
        start(middle, lambda: (o_rows(tile, 2, group), o_rows(tile, 3, group), oz_s.at[2], oz_r.at[3], in_dev))

    def o_end_own():
        arrived(inner, lambda: o_rows(tile, 2, 1 - group), ex_r.at[4])
        start(middle, lambda: (o_all.at[tile, 2], o_all.at[tile, 2], oc_s.at[0, 2], oc_r.at[0, 2], p_dev))

    def o_end_over():
        arrived(inner, lambda: o_all.at[over, 2], oz_r.at[0])
        start(middle, lambda: (o_all.at[over, 2], o_all.at[over, 2], oc_s.at[1, 2], oc_r.at[1, 2], p_dev))

    def o_chain(kind):
        arrived(inner, lambda: o_rows(tile, kind, group), oz_r.at[kind])
        start(middle, lambda: (o_rows(tile, kind, group), o_rows(tile, kind, group), ox_s.at[kind], ox_r.at[kind], x_dev))
        start(middle, lambda: (o_rows(tile, kind, group), o_rows(tile, kind, group), oy_s.at[0, kind], oy_r.at[0, kind], y_dev))

    def o_over(kind):
        arrived(inner, lambda: o_rows(over, kind, group), ox_r.at[kind])
        if kind != 1:
            start(middle, lambda: (
                o_rows(over, kind, group), o_rows(over, kind, group), oy_s.at[1, kind], oy_r.at[1, kind], y_dev))

    def o_peer(kind):
        arrived(inner, lambda: o_rows(tile, kind, 1 - group), oy_r.at[0, kind])
        if kind == 1:
            start(middle, lambda: (
                o_rows(tile, kind, 1 - group), o_rows(tile, kind, 1 - group), oy_s.at[1, kind], oy_r.at[1, kind], x_dev))
        start(middle, lambda: (
            o_all.at[tile, kind], o_all.at[tile, kind], oc_s.at[0, kind], oc_r.at[0, kind], p_dev))

    def o_last(kind):
        arrived(inner, lambda: o_rows(over, kind, 1 - group), oy_r.at[1, kind])
        start(middle, lambda: (
            o_all.at[over, kind], o_all.at[over, kind], oc_s.at[1, kind], oc_r.at[1, kind], p_dev))

    q_over(0)
    for at in range(1, chunks):
        if at == chunks - 1:
            tokens(1)
            o_first()
        q_over(at)
        q_peer(at - 1)
    q_peer(chunks - 1)
    for load in loads:
        load.wait()
    arrived(None, lambda: w_block(mate), qo_r)
    for part in (0, 1):
        for at in range(chunks):
            arrived(None, lambda: w_rows(mate_over, part, at), qc_r.at[part, at])

    strip = 32

    def norm_of(row):
        def norm(at, carry):
            rows = pl.ds(pl.multiple_of(at * strip, strip), strip)
            given = n_all[row, rows, :].astype(jnp.float32)
            normed[rows, :] = (layer_norm(given) * (1.0 + modulation[1:2]) + modulation[0:1]).astype(normed.dtype)
            return carry

        lax.fori_loop(0, block // strip, norm, 0)

    def project(row, pair, extra=False):
        place_of = pl.ds(pl.multiple_of(row * block, block), block)
        weights = w_more[...] if extra else w_all[:, pl.ds(pl.multiple_of(pair * (6 * HD), 128), 6 * HD)]
        part = jnp.dot(normed[...], weights, preferred_element_type=jnp.float32)
        for at in (0, 1):
            here = 3 * HD * at
            queries[2 * pair + at, place_of, :] = root_norm(part[:, here : here + HD]).astype(queries.dtype)
            keys[2 * pair + at, place_of, :] = root_norm(part[:, here + HD : here + 2 * HD]).astype(keys.dtype)
            values[2 * pair + at, place_of, pl.ds(0, HD)] = part[:, here + 2 * HD : here + 3 * HD].astype(values.dtype)

    final = (seqs - 1) * (1 - side)

    def in_order(step, carry):
        @pl.when(step == 1)
        def _():
            o_over(0)
            more()
            o_end()

        @pl.when(step == 2)
        def _():
            tokens(2)

        far, way = (step + 1) // 2, (step + 1) % 2
        row = place + far * (2 * way - 1)

        @pl.when(both(both(row >= 0, row < seqs), row != final))
        def _():
            norm_of(row)
            lax.fori_loop(0, pairs, lambda pair, carry: (project(row, pair), carry)[1], 0)

        return carry

    lax.fori_loop(0, 2 * seqs - 3, in_order, 0)
    o_end_far()
    o_last(0)
    tokens(3)
    norm_of(final)

    def leave(step, turn):
        extra = step // pairs
        row = (turn + 2 * (1 - side)) % seqs
        target, slot = row // 2 + 1, 1 - ((row + 1) // 2) % 2
        kind = (side != row // 2).astype(jnp.int32) + 2 * (extra + outer_end.astype(jnp.int32))
        source = attended.at[step, pl.ds(pl.multiple_of(row * block, block), block)]
        landing = att_in.at[kind, step - extra, pl.ds(pl.multiple_of(slot * block, block), block)]
        got = at_r.at[kind, slot, step - extra]

        def away():
            return copy(source, landing, at_s.at[turn, step], got, {"seq": target})

        def stay():
            return pltpu.make_async_copy(source, landing, got)

        return row, place != target, away, stay

    def attend(step):
        for turn in range(seqs):
            row, far, away, stay = leave(step, turn)
            at = pl.ds(pl.multiple_of(row * block, block), block)
            for half in (0, 1):
                head = 2 * (step % pairs) + half
                scores = lax.dot_general(
                    queries[head, at, :], keys[head], (((1,), (1,)), ((), ())), preferred_element_type=jnp.float32
                )
                expo = jnp.exp2(scores * scale).astype(jnp.bfloat16)
                mixed = jnp.dot(expo, values[head], preferred_element_type=jnp.float32)
                attended[step, at, pl.ds(half * HD, HD)] = (mixed[:, :HD] * (1.0 / mixed[:, HD:])).astype(attended.dtype)
            run(far, lambda away=away: away().start())
            run(jnp.logical_not(far), lambda stay=stay: stay().start())

    def mine(step):
        return jnp.logical_or(inner, step < pairs - 1)

    def one_more(step, carry):
        row = (final + step) % seqs

        @pl.when(step == 1)
        def _():
            o_chain(3)
            o_over(1)
            o_peer(1)

        @pl.when(step > 0)
        def _():
            norm_of(row)

        project(row, 0, True)
        return carry

    def one_pair(step, carry):
        @pl.when(both(mine(step), step < pairs))
        def _():
            project(final, step)

        @pl.when(both(inner, step == pairs))
        def _():
            copy(more_block(mate), more_block(mate), ex_s.at[2], ex_r.at[2], p_dev).wait_recv()
            copy(more_block(mate_over), more_block(mate_over), ex_s.at[3], ex_r.at[3], p_dev).wait_recv()
            lax.fori_loop(0, seqs, one_more, 0)
            o_over(3)
            o_peer(3)

        @pl.when(mine(step))
        def _():
            attend(step)

        @pl.when(step == 0)
        def _():
            o_chain(1)
            o_end_own()

        @pl.when(step == 1)
        def _():
            more_over()

        return carry

    lax.fori_loop(0, pairs + 1, one_pair, 0)
    o_end_over()

    run(inner, load_o.wait)

    def rows_here(kind):
        copy(o_all.at[mate, kind], o_all.at[mate, kind], oc_s.at[0, kind], oc_r.at[0, kind], p_dev).wait_recv()
        copy(o_all.at[mate_over, kind], o_all.at[mate_over, kind], oc_s.at[1, kind], oc_r.at[1, kind], p_dev).wait_recv()

    def attended_here(kind, slot, pair):
        landing = att_in.at[kind, pair, pl.ds(slot * block, block)]
        copy(landing, landing, at_r.at[kind, slot, pair], at_r.at[kind, slot, pair], p_dev).wait_recv()

    def add_up(kind, which, fresh=False):
        cut = 2 if wo.shape[1] % 256 == 0 else 1
        wide = wo.shape[1] // cut

        def columns(at, carry):
            owner, some = at // cut, pl.ds(pl.multiple_of(at % cut * wide, 128), wide)
            here = pl.ds(pl.multiple_of(at * wide, 128), wide)
            total = 0.0 if fresh else summed[:, here]
            for pair in which:
                rows = pl.ds(pl.multiple_of(pair * 2 * HD, 2 * HD), 2 * HD)
                total += jnp.dot(att_in[kind, pair], o_all[owner, kind, rows, some], preferred_element_type=jnp.float32)
            summed[:, here] = total
            return carry

        lax.fori_loop(0, cut * o_all.shape[0], columns, 0)

    @pl.when(inner)
    def _():
        rows_here(0)
        for slot in (0, 1):
            for pair in range(pairs):
                landing = att_in.at[0, pair, pl.ds(slot * block, block)]
                pltpu.make_async_copy(attended.at[pair, pl.ds(0, block)], landing, at_r.at[0, slot, pair]).wait()
        add_up(0, range(pairs), True)

    def from_end(pair, kind):
        for slot in (0, 1):
            attended_here(kind, slot, pair)
        add_up(kind, [pair])

    @pl.when(inner)
    def _():
        rows_here(2)
        for slot in (0, 1):
            landing = att_in.at[2, pairs - 1, pl.ds(slot * block, block)]
            pltpu.make_async_copy(attended.at[pairs, pl.ds(0, block)], landing, at_r.at[2, slot, pairs - 1]).wait()
        add_up(2, [pairs - 1])
        from_end(0, 2)

    o_last(1)
    o_last(3)

    @pl.when(inner)
    def _():
        rows_here(1)
        for pair in range(pairs):
            for slot in (0, 1):
                attended_here(1, slot, pair)
        add_up(1, range(pairs))
        rows_here(3)
        for slot in (0, 1):
            attended_here(3, slot, pairs - 1)
            attended_here(3, slot, 0)
        add_up(3, [0, pairs - 1])

        def later(at, carry):
            from_end(1 + at // 2, 2 + at % 2)
            return carry

        lax.fori_loop(0, 2 * (pairs - 2), later, 0)

    def message(slot):
        return copy(msg.at[slot], msg_in.at[1 - slot], ms_s.at[slot], ms_r.at[1 - slot], j_dev)

    def answer():
        return copy(result, result, rs_s, rs_r, out_dev)

    channels = latent.shape[0]

    def level(offset):
        at = jnp.broadcast_to(index[...].astype(jnp.float32), (1, block)) + offset
        return noise_level(at, NSTEPS)

    @pl.when(inner)
    def _():
        copy(latent, lat_in, ln_s, ln_r, p_dev).wait_recv()
        copy(weight, wt_in, wt_s, wt_r, p_dev).wait_recv()
        now, after = level(0.0), level(1.0)
        for slot in (0, 1):
            row = place - toward * slot

            def norm(at, carry):
                rows = pl.ds(pl.multiple_of(at * strip, strip), strip)
                sums = pl.ds(pl.multiple_of(slot * block + at * strip, strip), strip)
                mixed = n_all[row, rows, :].astype(jnp.float32) + modulation[2:3] * summed[sums, :]
                normed[rows, :] = (layer_norm(mixed) * (1.0 + modulation[4:5]) + modulation[3:4]).astype(normed.dtype)
                return carry

            lax.fori_loop(0, block // strip, norm, 0)
            velocity = lax.dot_general(
                w_head[...], normed[...], (((1,), (1,)), ((), ())), preferred_element_type=jnp.float32
            )
            base = (latent if slot == 0 else lat_in)[...]
            weighs = (weight if slot == 0 else wt_in)[...].astype(jnp.float32)
            joint[slot, pl.ds(0, channels), :] = (base + (after - now) * velocity) * weighs
            joint[slot, pl.ds(channels, channels), :] = (base - now * velocity) * weighs
            msg[slot, pl.ds(0, 2 * channels), :] = joint[slot].astype(msg.dtype)
            msg[slot, pl.ds(2 * channels, 16), :] = jnp.broadcast_to(weighs, (16, block)).astype(msg.dtype)
            run(paired, lambda slot=slot: message(slot).start())

        @pl.when(jnp.logical_not(paired))
        def _():
            msg_in[...] = jnp.zeros_like(msg_in)

        for slot in (1, 0):
            run(paired, lambda slot=slot: message(1 - slot).wait_recv())
            weighs = (weight if slot == 0 else wt_in)[...].astype(jnp.float32)
            given = msg_in[slot].astype(jnp.float32)
            joined = (joint[slot] + given[: 2 * channels]) / (weighs + given[2 * channels : 2 * channels + 1])
            if slot == 1:
                joint[1] = joined
                copy(joint.at[1], result, rs_s, rs_r, out_dev).start()
            else:
                joined_out[...] = joined
        for slot in (1, 0):
            run(paired, lambda slot=slot: message(slot).wait_send())
        copy(joint.at[1], result, rs_s, rs_r, out_dev).wait_send()

    @pl.when(outer_end)
    def _():
        answer().wait_recv()
        joined_out[...] = result[...]

    def drain(step, carry):
        for turn in range(seqs):
            _, far, away, _ = leave(step, turn)
            run(both(far, mine(step)), lambda away=away: away().wait_send())
        return carry

    lax.fori_loop(0, pairs + 1, drain, 0)
    for cond, make in sent:
        run(cond(), lambda make=make: copy(*make()).wait_send())


def fused(hidden, wq, wo, modulation, w_head, latent, weight, index):
    tiles, seqs = lax.axis_size("tile"), lax.axis_size("seq")
    block, width = hidden.shape
    length, heads = seqs * block, wq.shape[1] // (3 * HD)
    pairs, chunks = heads // 2, 3
    channels = w_head.shape[0]
    sizes = [(2, seqs)] * 2 + [(chunks,)] * 4 + [(2, chunks)] * 2 + [()] * 2 + [(4,)] * 4 + [(2, 4)] * 4 + [(5,)] * 2
    sizes += [(seqs, pairs + 1), (4, 2, pairs)] + [()] * 4 + [(2,)] * 2 + [()] * 2
    any_space, vmem = pl.BlockSpec(memory_space=pl.ANY), pl.BlockSpec(memory_space=pltpu.VMEM)
    return pl.pallas_call(
        functools.partial(step_kernel, math.log2(math.e) / math.sqrt(HD)),
        out_shape=jax.ShapeDtypeStruct((2 * channels, block), jnp.float32),
        in_specs=[any_space] * 5 + [vmem] * 3,
        out_specs=vmem,
        scratch_shapes=[
            pltpu.VMEM((seqs, block, width), hidden.dtype),
            pltpu.VMEM((block, width), hidden.dtype),
            pltpu.VMEM((tiles * wq.shape[0], wq.shape[1]), wq.dtype),
            pltpu.VMEM((tiles * wq.shape[0], 6 * HD), wq.dtype),
            pltpu.VMEM((heads, length, HD), hidden.dtype),
            pltpu.VMEM((heads, length, HD), hidden.dtype),
            pltpu.VMEM((heads, length, 2 * HD), hidden.dtype),
            pltpu.VMEM((pairs + 1, length, 2 * HD), hidden.dtype),
            pltpu.VMEM((4, pairs, 2 * block, 2 * HD), hidden.dtype),
            pltpu.VMEM((tiles, 4) + wo.shape, wo.dtype),
            pltpu.VMEM((2 * block, width), jnp.float32),
            pltpu.VMEM(modulation.shape, modulation.dtype),
            pltpu.VMEM(w_head.shape, w_head.dtype),
            pltpu.VMEM((channels, block), jnp.float32),
            pltpu.VMEM((1, block), jnp.int32),
            pltpu.VMEM((2, 2 * channels, block), jnp.float32),
            pltpu.VMEM((2, 2 * channels + 16, block), jnp.bfloat16),
            pltpu.VMEM((2, 2 * channels + 16, block), jnp.bfloat16),
            pltpu.VMEM((2 * channels, block), jnp.float32),
            pltpu.SemaphoreType.DMA((5,)),
        ]
        + [pltpu.SemaphoreType.DMA(shape) for shape in sizes],
        compiler_params=pltpu.CompilerParams(collective_id=1, has_side_effects=True, vmem_limit_bytes=67043328),
    )(hidden, wq, wo, modulation, w_head, latent, weight, index)


def fits(hidden, w_qkv, w_out):
    sizes = tuple(lax.axis_size(name) for name in ("group", "tile", "seq"))
    heads = w_qkv.shape[1] // (3 * HD)
    return sizes == (2, 4, 4) and heads % 2 == 0 and heads >= 4 and w_out.shape[1] % 128 == 0 and w_qkv.shape[0] % 96 == 0


def spread(hidden, modulation, w_qkv, w_out, w_head):
    local = hidden[0].astype(jnp.float32)
    norm_in = (layer_norm(local) * (1.0 + modulation[1]) + modulation[0]).astype(jnp.bfloat16)
    _, out_blocks, attended = gather(norm_in, w_qkv, w_out)
    attended = lax.all_to_all(attended, "seq", split_axis=0, concat_axis=1, tiled=True)
    out_blocks = out_blocks.reshape(out_blocks.shape[0], -1, out_blocks.shape[3])
    return tail(attended, out_blocks, hidden[0], modulation, w_head)


def shards(hidden, modulation, w_qkv, w_out, w_head, latent, weights_int, step_index):
    if fits(hidden, w_qkv, w_out):
        joined = fused(hidden[0], w_qkv, w_out, modulation, w_head.T, latent[0].T, weights_int, step_index[None])
        channels = latent.shape[2]
        return (joined[:channels].T[None], joined[channels:].T[None])
    velocity = spread(hidden, modulation, w_qkv, w_out, w_head).T
    index = step_index[0].astype(jnp.float32)
    now = noise_level(index, NSTEPS)
    after = noise_level(index + 1.0, NSTEPS)
    base = latent[0].T
    weight = weights_int[0].astype(jnp.float32)
    moved = base + (after - now) * velocity
    guess = base - now * velocity
    weighted = jnp.concatenate([moved, guess], axis=0) * weight[None, :]
    seq_count, tile_count = lax.axis_size("seq"), lax.axis_size("tile")
    jump = seq_count - 2
    moves = [
        (t * seq_count + s, (t + 1) * seq_count + s - jump)
        for t in range(tile_count - 1)
        for s in range(jump, seq_count)
    ]
    moves = moves + [(there, here) for here, there in moves]
    other_sums = lax.ppermute(weighted.astype(jnp.bfloat16), ("tile", "seq"), moves)
    other_weight = lax.ppermute(weight.astype(jnp.bfloat16), ("tile", "seq"), moves)
    totals = weighted + other_sums.astype(jnp.float32)
    norms = weight + other_weight.astype(jnp.float32)
    joined = totals / norms[None, :]
    channels = velocity.shape[0]
    return (joined[:channels].T[None], joined[channels:].T[None])


def solution(mesh):
    in_specs = (
        P(("group", "tile"), "seq", None),
        P("group", None),
        P("tile", "seq"),
        P("seq", "tile"),
        P(),
        P(("group", "tile"), "seq", None),
        P(("group", "tile"), "seq"),
        P("group"),
    )
    out_specs = (P(("group", "tile"), "seq", None), P(("group", "tile"), "seq", None))
    return jax.shard_map(shards, mesh=mesh, in_specs=in_specs, out_specs=out_specs, check_vma=False)
```
